768 devices in a mesh: gx: 12 (over z), gy: 64 (over y, x, core).
Axes of the slice: x: 4, y: 8, z: 12, core: 2. Of those that a mesh axis runs over, the one named last changes fastest.
Arguments:
- ensemble: float32 [288, 4096, 128], P('gx', 'gy'), may hold values from -30 to 30
- coefficients: float32 [3, 288, 4096], P(None, 'gx', 'gy'), may hold values from -0.3 to 0.3
- obs_owner: int32 [1024], replicated, may hold values from 0 to 767, as said below
- obs_cell: int32 [1024], replicated, may hold values from 0 to 1535
- obs_batch: int32 [1024], replicated, may hold values from 0 to 1, as said below
- obs_value: float32 [1024], replicated, may hold values from -6 to 6
- obs_var: float32 [1024], replicated, may hold values from 0.5 to 5
Outputs:
- analysis: float32 [288, 4096, 128], P('gx', 'gy')
The draws below stay inside these ranges and needn't reach their ends.
Inputs may be any that keep to these rules, and one draw needn't show every extreme that they name: Exactly 512 observations have obs_batch 0 and 512 have 1; in each batch no tile owns more than 2 observations and some tile owns exactly 2. `obs_owner`: owner tiles are numbered by the first tile index times 64 plus the second.
All inputs are finite; a program needn't handle non-finite values.
Results may differ from the reference program's by a relative error of at most 0.00014.
Values sent between devices are 32-bit elements; how exact they have to be, the bound alone decides.
No kernel may reach another device: no remote copies, remote signals or barrier semaphores. Data moves between devices by JAX's collectives and lax.ppermute only.
A program may use at most 32 MiB of HBM per device.

```python
import math
import jax
import jax.numpy as jnp
from jax import lax

M = 128
CX = 24
CY = 64
STEPS = 4
CAP = 2
NX = 288
NY = 4096
NB = 512
NOBS = 1024
N_GX = 12
N_GY = 64


def observation_plan(key):
    devices = N_GX * N_GY
    slot_count = devices * CAP
    owners = []
    for batch in range(2):
        batch_key = jax.random.fold_in(key, 11 + batch)
        key_heavy, key_noise, key_star = jax.random.split(batch_key, 3)
        heavy = jax.random.randint(key_heavy, (devices,), 0, 4)
        noise = jax.random.randint(key_noise, (slot_count,), 0, 1000)
        star = jax.random.randint(key_star, (), 0, devices)
        slots = jnp.arange(slot_count)
        tiles = slots // CAP
        score = (heavy[tiles] * 1000 + noise) * slot_count + slots
        score = score + jnp.where(tiles == star, 8000 * slot_count, 0)
        score = score + jnp.where((slots == 0) | (slots == slot_count - CAP), 4000 * slot_count, 0)
        chosen = lax.top_k(score.astype(jnp.int32), NB)[1]
        owners.append((chosen // CAP).astype(jnp.int32))
    owner = jnp.concatenate(owners)
    batch_ids = jnp.concatenate([jnp.zeros((NB,), jnp.int32), jnp.ones((NB,), jnp.int32)])
    shuffle = jax.random.permutation(jax.random.fold_in(key, 29), 2 * NB)
    return (owner[shuffle], batch_ids[shuffle])


def draw_obs_owner(key, part):
    return observation_plan(key)[0]


def draw_obs_batch(key, part):
    return observation_plan(key)[1]


def draw_coefficients(key, part):
    key_diff, key_speed = jax.random.split(jax.random.fold_in(key, 5))
    diffuse = jnp.exp(jax.random.uniform(key_diff, (1, NX, NY), jnp.float32, jnp.log(0.05), jnp.log(0.2)))
    speeds = jax.random.uniform(key_speed, (2, NX, NY), jnp.float32, -0.3, 0.3)
    return jnp.concatenate([diffuse, speeds], 0)


def draw_ensemble(key, part):
    key_base, key_scale = jax.random.split(jax.random.fold_in(key, 7), 2)
    base = jnp.clip(jax.random.normal(key_base, (NX, NY, M), jnp.float32), -6.0, 6.0)
    cell_scale = jnp.exp(jax.random.uniform(key_scale, (NX, NY, 1), jnp.float32, jnp.log(0.4), jnp.log(4.0)))
    values = base * cell_scale
    return jnp.clip(values, -30.0, 30.0)


def place_ends(values, key, least, high):
    extent = values.shape
    place = [jax.random.randint(jax.random.fold_in(key, axis), (), 0, extent[axis]) for axis in range(len(extent))]
    values = values.at[tuple(place)].set(least)
    longest = extent.index(max(extent))
    place[longest] = (place[longest] + 1) % extent[longest]
    return values.at[tuple(place)].set(high)


def gaussian(stream_key, dims, width, most, kind=jnp.bfloat16):
    values = width * jax.random.normal(stream_key, dims, jnp.float32)
    return jnp.clip(values, min=-most, max=most).astype(kind)


def setup_inputs(seed: int = 0) -> dict:
    seeds = jax.random.split(jax.random.key(seed), 8)
    return {
        "ensemble": draw_ensemble(jax.random.fold_in(seeds[7], 71), 0),
        "coefficients": draw_coefficients(jax.random.fold_in(seeds[7], 71), 0),
        "obs_owner": draw_obs_owner(jax.random.fold_in(seeds[7], 71), 0),
        "obs_cell": place_ends(jax.random.randint(seeds[3], (NOBS,), 0, CX * CY), jax.random.fold_in(seeds[3], 1), 0, (CX * CY) - 1).astype(jnp.int32),
        "obs_batch": draw_obs_batch(jax.random.fold_in(seeds[7], 71), 0),
        "obs_value": gaussian(seeds[5], (NOBS,), 1.0, 6.0, jnp.float32),
        "obs_var": jnp.clip(jnp.exp(jax.random.uniform(seeds[6], (NOBS,), jnp.float32, math.log(0.5), math.log(5.0))), 0.5, 5.0),
    }


EPS = 1e-05

def advance(field, diffuse, speed_x, speed_y):
    padded = jnp.pad(field, ((1, 1), (1, 1), (0, 0)))
    east_side = padded[2:, 1:-1]
    west_side = padded[:-2, 1:-1]
    north_side = padded[1:-1, 2:]
    south_side = padded[1:-1, :-2]
    spread = east_side + west_side + north_side + south_side - 4.0 * field
    carried = 0.5 * (speed_x[..., None] * (east_side - west_side) + speed_y[..., None] * (north_side - south_side))
    return field + diffuse[..., None] * spread - (1.0 + 0.5 * jnp.tanh(field)) * carried

def chol_solve(factor, rhs):
    first = lax.linalg.triangular_solve(factor, rhs, left_side=True, lower=True)
    return lax.linalg.triangular_solve(factor, first, left_side=True, lower=True, transpose_a=True)

def assimilate(field, owner, cell, value, variance):
    devices = N_GX * N_GY
    pos_x = owner // N_GY * CX + cell // CY
    pos_y = owner % N_GY * CY + cell % CY
    prior = field[pos_x, pos_y]
    mean_prior = jnp.mean(prior, 1)
    anomaly = prior - mean_prior[:, None]
    scaled = anomaly / variance[:, None]
    outer = scaled[:, :, None] * anomaly[:, None, :]
    gram = jax.ops.segment_sum(outer, owner, num_segments=devices)
    rhs = jax.ops.segment_sum(scaled * (value - mean_prior)[:, None], owner, num_segments=devices)
    system = gram + (M - 1) * jnp.eye(M, dtype=jnp.float32)
    factor = jnp.linalg.cholesky(system)
    solved = chol_solve(factor, gram)
    weights = chol_solve(factor, rhs[..., None])[..., 0]
    change = jnp.sum(anomaly * weights[owner], 1)[:, None] - 0.5 * jnp.einsum('km,kmn->kn', anomaly, solved[owner], precision=lax.Precision.HIGHEST)
    gain = anomaly / (jnp.sum(anomaly * anomaly, 1) + EPS)[:, None]
    where_x = pos_x.astype(jnp.float32)
    where_y = pos_y.astype(jnp.float32)
    reach_x = NX / 2.0
    reach_y = NY / 2.0
    members_mean = jnp.mean(field, 2, keepdims=True)
    spreads = field - members_mean
    coord_y = jnp.arange(NY).astype(jnp.float32)

    def one_row(args):
        line, coord_x = args
        covary = jnp.dot(line, gain.T, precision=lax.Precision.HIGHEST)
        delta_x = coord_x - where_x[None, :]
        delta_y = coord_y[:, None] - where_y[None, :]
        taper = jnp.exp(-0.5 * (delta_x * delta_x / (reach_x * reach_x) + delta_y * delta_y / (reach_y * reach_y)))
        return jnp.dot(taper * covary, change, precision=lax.Precision.HIGHEST)
    increment = lax.map(one_row, (spreads, jnp.arange(NX).astype(jnp.float32)))
    return field + increment

def reference(ensemble, coefficients, obs_owner, obs_cell, obs_batch, obs_value, obs_var):
    field = ensemble
    for counter in range(STEPS):
        field = advance(field, coefficients[0], coefficients[1], coefficients[2])
    ordering = jnp.argsort(obs_batch, stable=True).astype(jnp.int32)
    for batch in range(2):
        picked = ordering[batch * NB:(batch + 1) * NB]
        field = assimilate(field, obs_owner[picked], obs_cell[picked], obs_value[picked], obs_var[picked])
    return field
```

```python
import functools

import jax
import jax.numpy as jnp
from jax import lax
from jax.experimental import pallas as pl
from jax.experimental.pallas import tpu as pltpu
from jax.sharding import PartitionSpec as P

STEPS = 4
CAP = 2
BATCHES = 2
EPS = 1e-05
GY_FACTORS = {64: (8, 4, 2), 8: (2, 2, 2)}


def neighbours(axis):
    size = lax.axis_size(axis)
    up = [(i, i + 1) for i in range(size - 1)]
    return up, [(j, i) for i, j in up]


def with_halo(value, axis, dim, width):
    up, down = neighbours(axis)
    length = value.shape[dim]
    before = lax.ppermute(lax.slice_in_dim(value, length - width, length, axis=dim), axis, up)
    after = lax.ppermute(lax.slice_in_dim(value, 0, width, axis=dim), axis, down)
    return jnp.concatenate([before, value, after], axis=dim)


def advance(padded, diffuse, speed_x, speed_y):
    centre = padded[1:-1, 1:-1]
    east_side = padded[2:, 1:-1]
    west_side = padded[:-2, 1:-1]
    north_side = padded[1:-1, 2:]
    south_side = padded[1:-1, :-2]
    spread = east_side + west_side + north_side + south_side - 4.0 * centre
    carried = 0.5 * (
        speed_x[..., None] * (east_side - west_side)
        + speed_y[..., None] * (north_side - south_side)
    )
    return centre + diffuse[..., None] * spread - (1.0 + 0.5 * jnp.tanh(centre)) * carried


def share(rows, axis, count, groups=None):
    height, width = rows.shape
    copies = jnp.broadcast_to(rows[None], (count, height, width)).reshape(count * height, width)
    return lax.all_to_all(copies, axis, 0, 0, axis_index_groups=groups, tiled=True)


def share_all(rows):
    ys, xs, cs = GY_FACTORS[lax.axis_size("gy")]

    def at(y, x, c):
        return (y * xs + x) * cs + c

    along_y = [[at(y, x, c) for y in range(ys)] for x in range(xs) for c in range(cs)]
    along_x = [[at(y, x, c) for x in range(xs)] for y in range(ys) for c in range(cs)]
    along_c = [[at(y, x, c) for c in range(cs)] for y in range(ys) for x in range(xs)]
    rows = share(rows, "gx", lax.axis_size("gx"))
    rows = share(rows, "gy", ys, along_y)
    rows = share(rows, "gy", xs, along_x)
    return share(rows, "gy", cs, along_c)


def shared_row(owner, wide, narrow, slots):
    ys, xs, cs = GY_FACTORS[narrow]
    row, col = owner // narrow, owner % narrow
    y, x, c = col // (xs * cs), col // cs % xs, col % cs
    return (((c * xs + x) * ys + y) * wide + row) * slots


def local_cells(tile_id, obs_owner, obs_cell, obs_batch):
    span = 2048
    order = jnp.arange(obs_owner.shape[0], dtype=jnp.int32)
    key = order * span + obs_cell
    far = jnp.int32(obs_owner.shape[0] * span)
    cells = []
    for batch in range(BATCHES):
        mine = (obs_owner == tile_id) & (obs_batch == batch)
        first = jnp.min(jnp.where(mine, key, far))
        last = jnp.max(jnp.where(mine, key, -1))
        cells.append(jnp.where(first == far, 0, first % span))
        cells.append(jnp.where(last < 0, 0, last % span))
    return cells


def arrange(row_index, col_index, tile_x, tile_y, wide, narrow, owner, cell, batch, value, var):
    count = owner.shape[0]
    order = jnp.arange(count, dtype=jnp.int32)
    place = batch * (wide * narrow) + owner
    key = place * count + order
    ahead = key[:, None] < key[None, :]
    position = jnp.sum(ahead.astype(jnp.int32), 0)
    second = jnp.any(ahead & (place[:, None] == place[None, :]), 0)
    source = shared_row(owner, wide, narrow, BATCHES * CAP) + batch * CAP + second.astype(jnp.int32)
    px = owner // narrow * tile_x + cell // tile_y - row_index * tile_x
    py = owner % narrow * tile_y + cell % tile_y - col_index * tile_y
    pick = (position[None, :] == order[:, None]).astype(jnp.float32)
    table = jnp.stack(
        [
            source.astype(jnp.float32),
            place.astype(jnp.float32),
            px.astype(jnp.float32),
            py.astype(jnp.float32),
            value,
            var,
        ],
        0,
    )
    table = lax.dot_general(
        table, pick, (((1,), (1,)), ((), ())), precision=lax.Precision.HIGHEST
    )
    source = (table[0] + 0.5).astype(jnp.int32)
    place = table[1]
    edge = jnp.full((1,), -1.0, jnp.float32)
    follows = (place == jnp.concatenate([edge, place[:-1]])).astype(jnp.float32)
    leads = (place == jnp.concatenate([place[1:], edge])).astype(jnp.float32)

    def mate(row):
        zero = jnp.zeros((1,), jnp.float32)
        return leads * jnp.concatenate([row[1:], zero]) + follows * jnp.concatenate(
            [zero, row[:-1]]
        )

    rows = jnp.stack(
        [
            table[4],
            table[5],
            mate(table[4]),
            mate(table[5]) + (1.0 - leads - follows),
            leads,
            follows,
            table[2],
            table[3],
        ],
        0,
    )
    return source, rows


def split(value):
    high = value.astype(jnp.bfloat16)
    low = (value - high.astype(jnp.float32)).astype(jnp.bfloat16)
    return high, low


def assimilate_kernel(
    tile_x,
    tile_y,
    reach_x,
    reach_y,
    source_ref,
    rows_ref,
    cols_ref,
    shared_ref,
    field_ref,
    out_ref,
    obs_ref,
    gain_a,
    gain_b,
    change_a,
    change_b,
    taper_x,
    taper_y,
):
    count, members = obs_ref.shape
    half = count // BATCHES
    scale_x = -0.5 / (reach_x * reach_x)
    scale_y = -0.5 / (reach_y * reach_y)

    def fetch(index, carry):
        obs_ref[pl.ds(index, 1), :] = shared_ref[pl.ds(source_ref[index], 1), :]
        return carry

    lax.fori_loop(0, count, fetch, 0, unroll=8)

    def prepare(batch):
        low = batch * half
        prior = obs_ref[low : low + half, :]
        cols = cols_ref[low : low + half, :]
        value, var, mate_value, mate_var = (cols[:, i : i + 1] for i in range(4))
        leads, follows = cols[:, 4:5], cols[:, 5:6]
        mean = jnp.mean(prior, 1, keepdims=True)
        own = prior - mean
        after = pltpu.roll(prior, half - 1, 0)
        before = pltpu.roll(prior, 1, 0)
        mate_prior = jnp.where(leads > 0.0, after, before)
        mate_mean = jnp.mean(mate_prior, 1, keepdims=True)
        paired = leads + follows
        mate = (mate_prior - mate_mean) * paired
        own_own = jnp.sum(own * own, 1, keepdims=True)
        own_mate = jnp.sum(own * mate, 1, keepdims=True)
        rest = mate - own * (own_mate / jnp.maximum(own_own, 1e-30))
        area = own_own * jnp.sum(rest * rest, 1, keepdims=True)
        mate_mate = jnp.sum(mate * mate, 1, keepdims=True)
        floor = jnp.float32(members - 1)
        own_floor, mate_floor = floor * var, floor * mate_var
        det = own_floor * mate_floor + own_floor * mate_mate + mate_floor * own_own + area
        own_part = (mate_floor * own_own + area) / det
        mate_part = own_floor * own_mate / det
        shift = own_part * (value - mean) + mate_part * paired * (mate_value - mate_mean)
        change = shift - 0.5 * (own_part * own + mate_part * mate)
        gain = (own / (own_own + EPS)).T
        high, low_part = split(gain)
        gain_a[:members, :] = high
        gain_a[members:, :] = high
        gain_b[...] = low_part
        high, low_part = split(change)
        change_a[:, :members] = high
        change_a[:, members:] = low_part
        change_b[...] = high

    def increment(cells, taper):
        anomaly = cells - jnp.mean(cells, 1, keepdims=True)
        high, low = split(anomaly)
        covary = jnp.dot(
            jnp.concatenate([high, low], 1), gain_a[...], preferred_element_type=jnp.float32
        ) + jnp.dot(high, gain_b[...], preferred_element_type=jnp.float32)
        high, low = split(covary * taper)
        both = jnp.dot(high, change_a[...], preferred_element_type=jnp.float32)
        rest = jnp.dot(low, change_b[...], preferred_element_type=jnp.float32)
        return cells + (both[:, :members] + both[:, members:] + rest)

    def update_field(batch, from_ref):
        low = batch * half
        obs_x = rows_ref[6:7, low : low + half]
        obs_y = rows_ref[7:8, low : low + half]
        at_x = lax.broadcasted_iota(jnp.int32, (tile_x, half), 0).astype(jnp.float32) - obs_x
        at_y = lax.broadcasted_iota(jnp.int32, (tile_y, half), 0).astype(jnp.float32) - obs_y
        taper_x[...] = jnp.exp(scale_x * (at_x * at_x))
        taper_y[...] = jnp.exp(scale_y * (at_y * at_y))

        def one_row(index, carry):
            where = pl.ds(pl.multiple_of(index * tile_y, tile_y), tile_y)
            taper = taper_x[pl.ds(index, 1), :] * taper_y[...]
            out_ref[where, :] = increment(from_ref[where, :], taper)
            return carry

        lax.fori_loop(0, tile_x, one_row, 0, unroll=4)

    prepare(0)
    update_field(0, field_ref)
    chunk = min(half, 128)
    for start in range(half, count, chunk):
        gap_x = cols_ref[start : start + chunk, 6:7] - rows_ref[6:7, :half]
        gap_y = cols_ref[start : start + chunk, 7:8] - rows_ref[7:8, :half]
        taper = jnp.exp(scale_x * (gap_x * gap_x) + scale_y * (gap_y * gap_y))
        obs_ref[start : start + chunk, :] = increment(obs_ref[start : start + chunk, :], taper)
    prepare(1)
    update_field(1, out_ref)


def assimilate(source, rows, cols, shared, field, tile_x, tile_y, reach_x, reach_y):
    cells, members = field.shape
    count = source.shape[0]
    half = count // BATCHES
    vmem = pl.BlockSpec(memory_space=pltpu.VMEM)
    return pl.pallas_call(
        functools.partial(assimilate_kernel, tile_x, tile_y, reach_x, reach_y),
        name="assimilate",
        out_shape=jax.ShapeDtypeStruct((cells, members), jnp.float32),
        in_specs=[pl.BlockSpec(memory_space=pltpu.SMEM), vmem, vmem, vmem, vmem],
        out_specs=vmem,
        scratch_shapes=[
            pltpu.VMEM((count, members), jnp.float32),
            pltpu.VMEM((2 * members, half), jnp.bfloat16),
            pltpu.VMEM((members, half), jnp.bfloat16),
            pltpu.VMEM((half, 2 * members), jnp.bfloat16),
            pltpu.VMEM((half, members), jnp.bfloat16),
            pltpu.VMEM((tile_x, half), jnp.float32),
            pltpu.VMEM((tile_y, half), jnp.float32),
        ],
    )(source, rows, cols, shared, field)


def per_device(ensemble, coefficients, obs_owner, obs_cell, obs_batch, obs_value, obs_var):
    wide = lax.axis_size("gx")
    narrow = lax.axis_size("gy")
    row_index = lax.axis_index("gx")
    col_index = lax.axis_index("gy")
    tile_x, tile_y, members = ensemble.shape
    reach_x = tile_x * wide / 2.0
    reach_y = tile_y * narrow / 2.0
    field = with_halo(with_halo(ensemble, "gx", 0, STEPS), "gy", 1, STEPS)
    coefs = with_halo(with_halo(coefficients, "gx", 1, STEPS), "gy", 2, STEPS)
    source, rows = arrange(
        row_index,
        col_index,
        tile_x,
        tile_y,
        wide,
        narrow,
        obs_owner,
        obs_cell,
        obs_batch,
        obs_value,
        obs_var,
    )
    cells = local_cells(row_index * narrow + col_index, obs_owner, obs_cell, obs_batch)
    for _ in range(STEPS):
        coefs = coefs[:, 1:-1, 1:-1]
        field = advance(field, coefs[0], coefs[1], coefs[2])
    field = field.reshape(tile_x * tile_y, members)
    priors = jnp.concatenate([lax.dynamic_slice_in_dim(field, c, 1, 0) for c in cells], 0)
    shared = share_all(priors)
    field = assimilate(
        source, rows, rows.T, shared, field, tile_x, tile_y, reach_x, reach_y
    )
    return field.reshape(tile_x, tile_y, members)


def solution(mesh):
    placed = (P("gx", "gy", None), P(None, "gx", "gy"), P(), P(), P(), P(), P())
    return jax.shard_map(
        per_device, mesh=mesh, in_specs=placed, out_specs=P("gx", "gy", None), check_vma=False
    )
```

```python
import functools

import jax
import jax.numpy as jnp
from jax import lax
from jax.experimental import pallas as pl
from jax.experimental.pallas import tpu as pltpu
from jax.sharding import PartitionSpec as P

STEPS = 4
CAP = 2
GROUP = 12
BATCHES = 2
EPS = 1e-05
GY_FACTORS = {64: (8, 4, 2), 8: (2, 2, 2)}


def neighbours(axis):
    size = lax.axis_size(axis)
    up = [(i, i + 1) for i in range(size - 1)]
    return up, [(j, i) for i, j in up]


def with_halo(value, axis, dim, width):
    up, down = neighbours(axis)
    length = value.shape[dim]
    before = lax.ppermute(lax.slice_in_dim(value, length - width, length, axis=dim), axis, up)
    after = lax.ppermute(lax.slice_in_dim(value, 0, width, axis=dim), axis, down)
    return jnp.concatenate([before, value, after], axis=dim)


def advance(padded, diffuse, speed_x, speed_y):
    centre = padded[1:-1, 1:-1]
    east_side = padded[2:, 1:-1]
    west_side = padded[:-2, 1:-1]
    north_side = padded[1:-1, 2:]
    south_side = padded[1:-1, :-2]
    spread = east_side + west_side + north_side + south_side - 4.0 * centre
    carried = 0.5 * (
        speed_x[..., None] * (east_side - west_side)
        + speed_y[..., None] * (north_side - south_side)
    )
    return centre + diffuse[..., None] * spread - (1.0 + 0.5 * jnp.tanh(centre)) * carried


def share(rows, axis, count, groups=None):
    height, width = rows.shape
    copies = jnp.broadcast_to(rows[None], (count, height, width)).reshape(count * height, width)
    return lax.all_to_all(copies, axis, 0, 0, axis_index_groups=groups, tiled=True)


def share_all(rows):
    ys, xs, cs = GY_FACTORS[lax.axis_size("gy")]

    def at(y, x, c):
        return (y * xs + x) * cs + c

    along_y = [[at(y, x, c) for y in range(ys)] for x in range(xs) for c in range(cs)]
    along_x = [[at(y, x, c) for x in range(xs)] for y in range(ys) for c in range(cs)]
    along_c = [[at(y, x, c) for c in range(cs)] for y in range(ys) for x in range(xs)]
    rows = share(rows, "gx", lax.axis_size("gx"))
    rows = share(rows, "gy", ys, along_y)
    rows = share(rows, "gy", xs, along_x)
    return share(rows, "gy", cs, along_c)


def shared_row(owner, wide, narrow, slots):
    ys, xs, cs = GY_FACTORS[narrow]
    row, col = owner // narrow, owner % narrow
    y, x, c = col // (xs * cs), col // cs % xs, col % cs
    return (((c * xs + x) * ys + y) * wide + row) * slots


def local_cells(tile_id, obs_owner, obs_cell, obs_batch):
    span = 2048
    order = jnp.arange(obs_owner.shape[0], dtype=jnp.int32)
    key = (order * span + obs_cell)[None, :]
    batches = jnp.arange(BATCHES, dtype=jnp.int32)[:, None]
    mine = (obs_owner == tile_id)[None, :] & (obs_batch[None, :] == batches)
    first = jnp.min(jnp.where(mine, key, obs_owner.shape[0] * span), 1)
    last = jnp.max(jnp.where(mine, key, 0), 1)
    return jnp.stack([first, last], 1).reshape(-1) & (span - 1)


def arrange(row_index, col_index, tile_x, tile_y, wide, narrow, owner, cell, batch, value, var):
    count = owner.shape[0]
    order = jnp.arange(count, dtype=jnp.int32)
    place = batch * (wide * narrow) + owner
    key = place * count + order
    ahead = key[:, None] < key[None, :]
    position = jnp.sum(ahead.astype(jnp.int32), 0)
    second = jnp.any(ahead & (place[:, None] == place[None, :]), 0)
    source = shared_row(owner, wide, narrow, BATCHES * CAP) + batch * CAP + second.astype(jnp.int32)
    px = owner // narrow * tile_x + cell // tile_y - row_index * tile_x
    py = owner % narrow * tile_y + cell % tile_y - col_index * tile_y
    pick = (position[None, :] == order[:, None]).astype(jnp.float32)
    table = jnp.stack(
        [
            source.astype(jnp.float32),
            place.astype(jnp.float32),
            px.astype(jnp.float32),
            py.astype(jnp.float32),
            value,
            var,
        ],
        0,
    )
    table = lax.dot_general(
        table, pick, (((1,), (1,)), ((), ())), precision=lax.Precision.HIGHEST
    )
    source = (table[0] + 0.5).astype(jnp.int32)
    place = table[1]
    edge = jnp.full((1,), -1.0, jnp.float32)
    follows = (place == jnp.concatenate([edge, place[:-1]])).astype(jnp.float32)
    leads = (place == jnp.concatenate([place[1:], edge])).astype(jnp.float32)

    def mate(row):
        zero = jnp.zeros((1,), jnp.float32)
        return leads * jnp.concatenate([row[1:], zero]) + follows * jnp.concatenate(
            [zero, row[:-1]]
        )

    rows = jnp.stack(
        [
            table[4],
            table[5],
            mate(table[4]),
            mate(table[5]) + (1.0 - leads - follows),
            leads,
            follows,
            table[2],
            table[3],
        ],
        0,
    )
    return source, rows


def split(value):
    high = value.astype(jnp.bfloat16)
    low = (value - high.astype(jnp.float32)).astype(jnp.bfloat16)
    return high, low


def assimilate_kernel(
    tile_x,
    tile_y,
    reach_x,
    reach_y,
    source_ref,
    rows_ref,
    cols_ref,
    shared_ref,
    field_ref,
    out_ref,
    obs_ref,
    gain_a,
    gain_b,
    change_a,
    change_b,
    taper_x,
    taper_y,
):
    count, members = obs_ref.shape
    half = count // BATCHES
    scale_x = -0.5 / (reach_x * reach_x)
    scale_y = -0.5 / (reach_y * reach_y)

    def fetch(index, carry):
        obs_ref[pl.ds(index, 1), :] = shared_ref[pl.ds(source_ref[index], 1), :]
        return carry

    lax.fori_loop(0, count, fetch, 0, unroll=8)

    def prepare(batch):
        low = batch * half
        prior = obs_ref[low : low + half, :]
        cols = cols_ref[low : low + half, :]
        value, var, mate_value, mate_var = (cols[:, i : i + 1] for i in range(4))
        leads, follows = cols[:, 4:5], cols[:, 5:6]
        mean = jnp.mean(prior, 1, keepdims=True)
        own = prior - mean
        after = pltpu.roll(prior, half - 1, 0)
        before = pltpu.roll(prior, 1, 0)
        mate_prior = jnp.where(leads > 0.0, after, before)
        mate_mean = jnp.mean(mate_prior, 1, keepdims=True)
        paired = leads + follows
        mate = (mate_prior - mate_mean) * paired
        own_own = jnp.sum(own * own, 1, keepdims=True)
        own_mate = jnp.sum(own * mate, 1, keepdims=True)
        rest = mate - own * (own_mate / jnp.maximum(own_own, 1e-30))
        area = own_own * jnp.sum(rest * rest, 1, keepdims=True)
        mate_mate = jnp.sum(mate * mate, 1, keepdims=True)
        floor = jnp.float32(members - 1)
        own_floor, mate_floor = floor * var, floor * mate_var
        det = own_floor * mate_floor + own_floor * mate_mate + mate_floor * own_own + area
        own_part = (mate_floor * own_own + area) / det
        mate_part = own_floor * own_mate / det
        shift = own_part * (value - mean) + mate_part * paired * (mate_value - mate_mean)
        change = shift - 0.5 * (own_part * own + mate_part * mate)
        gain = (own / (own_own + EPS)).T
        high, low_part = split(gain)
        gain_a[:members, :] = high
        gain_a[members:, :] = high
        gain_b[...] = low_part
        high, low_part = split(change)
        change_a[:, :members] = high
        change_a[:, members:] = low_part
        change_b[...] = high

    def increment(cells, taper):
        anomaly = cells - jnp.mean(cells, 1, keepdims=True)
        high, low = split(anomaly)
        covary = jnp.dot(
            jnp.concatenate([high, low], 1), gain_a[...], preferred_element_type=jnp.float32
        ) + jnp.dot(high, gain_b[...], preferred_element_type=jnp.float32)
        high, low = split(covary * taper)
        both = jnp.dot(high, change_a[...], preferred_element_type=jnp.float32)
        rest = jnp.dot(low, change_b[...], preferred_element_type=jnp.float32)
        return cells + (both[:, :members] + both[:, members:] + rest)

    def update_field(batch, from_ref):
        low = batch * half
        obs_x = rows_ref[6:7, low : low + half]
        obs_y = rows_ref[7:8, low : low + half]
        at_x = lax.broadcasted_iota(jnp.int32, (tile_x, half), 0).astype(jnp.float32) - obs_x
        at_y = lax.broadcasted_iota(jnp.int32, (tile_y, half), 0).astype(jnp.float32) - obs_y
        taper_x[...] = jnp.exp(scale_x * (at_x * at_x))
        taper_y[...] = jnp.exp(scale_y * (at_y * at_y))

        for first in range(0, tile_x, GROUP):
            where = slice(first * tile_y, (first + GROUP) * tile_y)
            taper = jnp.concatenate(
                [taper_x[first + i : first + i + 1, :] * taper_y[...] for i in range(GROUP)], 0
            )
            out_ref[where, :] = increment(from_ref[where, :], taper)

    prepare(0)
    update_field(0, field_ref)
    chunk = min(half, 256)
    for start in range(half, count, chunk):
        gap_x = cols_ref[start : start + chunk, 6:7] - rows_ref[6:7, :half]
        gap_y = cols_ref[start : start + chunk, 7:8] - rows_ref[7:8, :half]
        taper = jnp.exp(scale_x * (gap_x * gap_x) + scale_y * (gap_y * gap_y))
        obs_ref[start : start + chunk, :] = increment(obs_ref[start : start + chunk, :], taper)
    prepare(1)
    update_field(1, out_ref)


def assimilate(source, rows, cols, shared, field, tile_x, tile_y, reach_x, reach_y):
    cells, members = field.shape
    count = source.shape[0]
    half = count // BATCHES
    vmem = pl.BlockSpec(memory_space=pltpu.VMEM)
    return pl.pallas_call(
        functools.partial(assimilate_kernel, tile_x, tile_y, reach_x, reach_y),
        name="assimilate",
        out_shape=jax.ShapeDtypeStruct((cells, members), jnp.float32),
        in_specs=[pl.BlockSpec(memory_space=pltpu.SMEM), vmem, vmem, vmem, vmem],
        out_specs=vmem,
        scratch_shapes=[
            pltpu.VMEM((count, members), jnp.float32),
            pltpu.VMEM((2 * members, half), jnp.bfloat16),
            pltpu.VMEM((members, half), jnp.bfloat16),
            pltpu.VMEM((half, 2 * members), jnp.bfloat16),
            pltpu.VMEM((half, members), jnp.bfloat16),
            pltpu.VMEM((tile_x, half), jnp.float32),
            pltpu.VMEM((tile_y, half), jnp.float32),
        ],
    )(source, rows, cols, shared, field)


def per_device(ensemble, coefficients, obs_owner, obs_cell, obs_batch, obs_value, obs_var):
    wide = lax.axis_size("gx")
    narrow = lax.axis_size("gy")
    row_index = lax.axis_index("gx")
    col_index = lax.axis_index("gy")
    tile_x, tile_y, members = ensemble.shape
    reach_x = tile_x * wide / 2.0
    reach_y = tile_y * narrow / 2.0
    field = with_halo(with_halo(ensemble, "gx", 0, STEPS), "gy", 1, STEPS)
    coefs = with_halo(with_halo(coefficients, "gx", 1, STEPS), "gy", 2, STEPS)
    cells = local_cells(row_index * narrow + col_index, obs_owner, obs_cell, obs_batch)
    for _ in range(STEPS):
        coefs = coefs[:, 1:-1, 1:-1]
        field = advance(field, coefs[0], coefs[1], coefs[2])
    field = field.reshape(tile_x * tile_y, members)
    priors = jnp.concatenate(
        [lax.dynamic_slice_in_dim(field, cells[i], 1, 0) for i in range(BATCHES * CAP)], 0
    )
    priors, obs_owner, obs_cell, obs_batch = lax.optimization_barrier(
        (priors, obs_owner, obs_cell, obs_batch)
    )
    source, rows = arrange(
        row_index,
        col_index,
        tile_x,
        tile_y,
        wide,
        narrow,
        obs_owner,
        obs_cell,
        obs_batch,
        obs_value,
        obs_var,
    )
    shared = share_all(priors)
    field = assimilate(
        source, rows, rows.T, shared, field, tile_x, tile_y, reach_x, reach_y
    )
    return field.reshape(tile_x, tile_y, members)


def solution(mesh):
    placed = (P("gx", "gy", None), P(None, "gx", "gy"), P(), P(), P(), P(), P())
    return jax.shard_map(
        per_device, mesh=mesh, in_specs=placed, out_specs=P("gx", "gy", None), check_vma=False
    )
```

```python
import functools

import jax
import jax.numpy as jnp
from jax import lax
from jax.experimental import pallas as pl
from jax.experimental.pallas import tpu as pltpu
from jax.sharding import PartitionSpec as P

STEPS = 4
CAP = 2
GROUP = 12
BATCHES = 2
EPS = 1e-05
GY_FACTORS = {64: (8, 4, 2), 8: (2, 2, 2)}


def neighbours(axis):
    size = lax.axis_size(axis)
    up = [(i, i + 1) for i in range(size - 1)]
    return up, [(j, i) for i, j in up]


def exchange(to_next, to_previous, axis):
    up, down = neighbours(axis)
    return lax.ppermute(to_next, axis, up), lax.ppermute(to_previous, axis, down)


def in_vmem():
    return pl.BlockSpec(memory_space=pltpu.VMEM)


def in_smem():
    return pl.BlockSpec(memory_space=pltpu.SMEM)


def grant(mib):
    return pltpu.CompilerParams(vmem_limit_bytes=mib << 20)


LINES = 8
MARGIN = 8


def pack_x_kernel(field_ref, coefs_ref, first_ref, last_ref, sems):
    tile_x, tile_y, _ = field_ref.shape
    kinds = coefs_ref.shape[0]
    copies = []
    for index, (out_ref, start) in enumerate(((first_ref, 0), (last_ref, tile_x - STEPS))):
        copies.append(
            pltpu.make_async_copy(
                field_ref.at[pl.ds(start, STEPS)], out_ref.at[:, pl.ds(0, tile_y)], sems.at[index]
            )
        )
        copies[-1].start()
    for out_ref, start in ((first_ref, 0), (last_ref, tile_x - STEPS)):
        out_ref[:, tile_y:, :] = jnp.zeros_like(out_ref[:, tile_y:, :])
        for kind in range(kinds):
            part = coefs_ref[kind, start : start + STEPS, :]
            for i in range(STEPS):
                out_ref[i, tile_y + kind : tile_y + kind + 1, :tile_y] = part[i : i + 1, :]
    for copy in copies:
        copy.wait()


def pack_x(field, coefs):
    tile_x, tile_y, members = field.shape
    slab = jax.ShapeDtypeStruct((STEPS, tile_y + LINES, members), jnp.float32)
    return pl.pallas_call(
        pack_x_kernel,
        name="pack_x",
        out_shape=(slab, slab),
        in_specs=[pl.BlockSpec(memory_space=pl.ANY), in_vmem()],
        out_specs=(in_vmem(), in_vmem()),
        scratch_shapes=[pltpu.SemaphoreType.DMA((2,))],
    )(field, coefs)


def pack_y_kernel(field_ref, coefs_ref, before_ref, after_ref, first_ref, last_ref):
    tile_x, tile_y, _ = field_ref.shape
    kinds = coefs_ref.shape[0]
    inner = slice(STEPS, STEPS + tile_x)
    outer = slice(STEPS + tile_x, 2 * STEPS + tile_x)
    for out_ref, start in ((first_ref, 0), (last_ref, tile_y - STEPS)):
        edge = slice(start, start + STEPS)
        out_ref[:STEPS, :STEPS, :] = before_ref[:, edge, :]
        out_ref[inner, :STEPS, :] = field_ref[:, edge, :]
        out_ref[outer, :STEPS, :] = after_ref[:, edge, :]
        out_ref[inner, STEPS:, :] = jnp.zeros_like(out_ref[inner, STEPS:, :])
        out_ref[:STEPS, STEPS:, :] = before_ref[:, tile_y : tile_y + LINES - STEPS, :]
        out_ref[outer, STEPS:, :] = after_ref[:, tile_y : tile_y + LINES - STEPS, :]
    for kind in range(kinds):
        part = coefs_ref[kind]
        for i in range(tile_x):
            for out_ref in (first_ref, last_ref):
                out_ref[STEPS + i, STEPS + kind : STEPS + kind + 1, :tile_y] = part[i : i + 1, :]


def pack_y(field, coefs, before, after):
    tile_x, tile_y, members = field.shape
    slab = jax.ShapeDtypeStruct((tile_x + 2 * STEPS, LINES, members), jnp.float32)
    return pl.pallas_call(
        pack_y_kernel,
        name="pack_y",
        out_shape=(slab, slab),
        in_specs=[in_vmem()] * 4,
        out_specs=(in_vmem(), in_vmem()),
        compiler_params=grant(8),
    )(field, coefs, before, after)


def advance(west, centre, east, diffuse, speed_x, speed_y):
    size = centre.shape[0]
    north = pltpu.roll(centre, size - 1, 0)
    south = pltpu.roll(centre, 1, 0)
    spread = east + west + north + south - 4.0 * centre
    carried = 0.5 * (speed_x * (east - west) + speed_y * (north - south))
    return centre + diffuse * spread - (1.0 + 0.5 * jnp.tanh(centre)) * carried


def look_kernel(
    copies,
    cells_ref,
    field_ref,
    coefs_ref,
    before_ref,
    after_ref,
    left_ref,
    right_ref,
    padded_ref,
    columns_ref,
    priors_ref,
    lines_ref,
    last_ref,
):
    tile_x, tile_y, members = field_ref.shape
    kinds = coefs_ref.shape[0]
    high_x, high_y = padded_ref.shape[0], padded_ref.shape[1]
    inner = slice(STEPS, STEPS + tile_x)
    outer = slice(STEPS + tile_x, high_x)
    own = slice(MARGIN, MARGIN + tile_y)
    padded_ref[:, :MARGIN, :] = jnp.zeros((high_x, MARGIN, members), jnp.float32)
    padded_ref[:, MARGIN + tile_y :, :] = jnp.zeros(
        (high_x, high_y - MARGIN - tile_y, members), jnp.float32
    )
    padded_ref[:STEPS, own, :] = before_ref[:, :tile_y, :]
    padded_ref[inner, own, :] = field_ref[...]
    padded_ref[outer, own, :] = after_ref[:, :tile_y, :]
    padded_ref[:, MARGIN - STEPS : MARGIN, :] = left_ref[:, :STEPS, :]
    padded_ref[:, MARGIN + tile_y : MARGIN + tile_y + STEPS, :] = right_ref[:, :STEPS, :]
    lane = lax.broadcasted_iota(jnp.int32, (high_x, members), 1)
    lines_ref[...] = jnp.zeros_like(lines_ref)
    for kind in range(kinds):
        base = kind * high_x
        lines_ref[base : base + STEPS, :] = before_ref[:, tile_y + kind, :]
        lines_ref[base + STEPS : base + STEPS + tile_x, :tile_y] = coefs_ref[kind]
        lines_ref[base + STEPS + tile_x : base + high_x, :] = after_ref[:, tile_y + kind, :]
        rows = slice(base, base + high_x)
        middle = pltpu.roll(lines_ref[rows, :], MARGIN, 1)
        left = pltpu.roll(left_ref[:, STEPS + kind, :], members + MARGIN - tile_y, 1)
        right = pltpu.roll(right_ref[:, STEPS + kind, :], MARGIN + tile_y, 1)
        line = jnp.where(lane < MARGIN, left, jnp.where(lane < MARGIN + tile_y, middle, right))
        near = (lane >= MARGIN - STEPS) & (lane < MARGIN + tile_y + STEPS)
        lines_ref[rows, :] = jnp.where(near, line, 0.0)
    columns_ref[...] = lines_ref[...].T
    width = 2 * STEPS + 1
    window = 24
    for slot in range(cells_ref.shape[0]):
        cell = cells_ref[slot]
        at_x = cell // tile_y
        at_y = cell % tile_y + (MARGIN - STEPS)
        start = pl.multiple_of(jnp.minimum(at_y // 8 * 8, high_y - window), 8)
        patch = [padded_ref[at_x + i, pl.ds(start, window), :] for i in range(width)]
        coefs = pltpu.roll(columns_ref[pl.ds(start, window), :], members - at_x, 1)
        for step in range(1, STEPS + 1):
            fresh = list(patch)
            for i in range(step, width - step):
                fresh[i] = advance(
                    patch[i - 1],
                    patch[i],
                    patch[i + 1],
                    *(coefs[:, k * high_x + i : k * high_x + i + 1] for k in range(kinds)),
                )
            patch = fresh
        last_ref[...] = patch[STEPS]
        prior = last_ref[pl.ds(at_y + STEPS - start, 1), :]
        for copy in range(copies):
            priors_ref[copy, slot : slot + 1, :] = prior


def look(copies, cells, field, coefs, before, after, left, right):
    tile_x, tile_y, members = field.shape
    high_x, high_y = tile_x + 2 * STEPS, tile_y + 2 * MARGIN
    return pl.pallas_call(
        functools.partial(look_kernel, copies),
        name="look",
        out_shape=(
            jax.ShapeDtypeStruct((high_x, high_y, members), jnp.float32),
            jax.ShapeDtypeStruct((members, members), jnp.float32),
            jax.ShapeDtypeStruct((copies, cells.shape[0], members), jnp.float32),
        ),
        in_specs=[in_smem()] + [in_vmem()] * 6,
        out_specs=(in_vmem(),) * 3,
        scratch_shapes=[
            pltpu.VMEM((members, members), jnp.float32),
            pltpu.VMEM((24, members), jnp.float32),
        ],
        compiler_params=grant(12),
    )(cells, field, coefs, before, after, left, right)


def forecast_kernel(kinds, padded_ref, columns_ref, out_ref, ping_ref, pong_ref, spread_ref):
    high_x, high_y, members = padded_ref.shape
    tile_x, tile_y = high_x - 2 * STEPS, high_y - 2 * MARGIN
    for index in range(kinds * high_x):
        spread_ref[index] = jnp.broadcast_to(
            columns_ref[:high_y, index : index + 1], (high_y, members)
        )
    source = padded_ref
    for step in range(1, STEPS + 1):
        final = step == STEPS
        target = (ping_ref, pong_ref)[step % 2]

        def one_row(x, carry):
            row = advance(
                source[x - 1],
                source[x],
                source[x + 1],
                *(spread_ref[kind * high_x + x] for kind in range(kinds)),
            )
            if final:
                where = pl.ds(pl.multiple_of((x - STEPS) * tile_y, tile_y), tile_y)
                out_ref[where, :] = row[MARGIN : MARGIN + tile_y]
            else:
                target[x] = row
            return carry

        lax.fori_loop(step, high_x - step, one_row, 0, unroll=2)
        source = target


def forecast(kinds, padded, columns):
    high_x, high_y, members = padded.shape
    tile_x, tile_y = high_x - 2 * STEPS, high_y - 2 * MARGIN
    work = STEPS * high_x * high_y * members
    return pl.pallas_call(
        functools.partial(forecast_kernel, kinds),
        name="forecast",
        out_shape=jax.ShapeDtypeStruct((tile_x * tile_y, members), jnp.float32),
        in_specs=[in_vmem()] * 2,
        out_specs=in_vmem(),
        scratch_shapes=[
            pltpu.VMEM((high_x, high_y, members), jnp.float32),
            pltpu.VMEM((high_x, high_y, members), jnp.float32),
            pltpu.VMEM((kinds * high_x, high_y, members), jnp.float32),
        ],
        compiler_params=grant(16),
        cost_estimate=pl.CostEstimate(
            flops=20 * work, bytes_accessed=8 * high_x * high_y * members, transcendentals=work
        ),
    )(padded, columns)


def share(rows, axis, count, groups=None):
    height, width = rows.shape
    copies = jnp.broadcast_to(rows[None], (count, height, width)).reshape(count * height, width)
    return lax.all_to_all(copies, axis, 0, 0, axis_index_groups=groups, tiled=True)


def share_all(copies):
    ys, xs, cs = GY_FACTORS[lax.axis_size("gy")]

    def at(y, x, c):
        return (y * xs + x) * cs + c

    along_y = [[at(y, x, c) for y in range(ys)] for x in range(xs) for c in range(cs)]
    along_x = [[at(y, x, c) for x in range(xs)] for y in range(ys) for c in range(cs)]
    across = [(i, i ^ 1) for i in range(ys * xs * cs)]
    rows = lax.all_to_all(copies, "gx", 0, 0, tiled=True)
    rows = rows.reshape(-1, rows.shape[-1])
    rows = share(rows, "gy", ys, along_y)
    rows = share(rows, "gy", xs, along_x)
    return rows, lax.ppermute(rows, "gy", across)


def shared_row(owner, side, wide, narrow, slots):
    ys, xs, cs = GY_FACTORS[narrow]
    row, col = owner // narrow, owner % narrow
    y, x, c = col // (xs * cs), col // cs % xs, col % cs
    return ((((c ^ side) * xs + x) * ys + y) * wide + row) * slots


def local_cells(tile_id, obs_owner, obs_cell, obs_batch):
    span = 2048
    order = jnp.arange(obs_owner.shape[0], dtype=jnp.int32)
    key = (order * span + obs_cell)[None, :]
    batches = jnp.arange(BATCHES, dtype=jnp.int32)[:, None]
    mine = (obs_owner == tile_id)[None, :] & (obs_batch[None, :] == batches)
    first = jnp.min(jnp.where(mine, key, obs_owner.shape[0] * span), 1)
    last = jnp.max(jnp.where(mine, key, 0), 1)
    return jnp.stack([first, last], 1).reshape(-1) & (span - 1)


def arrange(row_index, col_index, tile_x, tile_y, wide, narrow, owner, cell, batch, value, var):
    count = owner.shape[0]
    order = jnp.arange(count, dtype=jnp.int32)
    place = batch * (wide * narrow) + owner
    key = place * count + order
    ahead = key[:, None] < key[None, :]
    position = jnp.sum(ahead.astype(jnp.int32), 0)
    second = jnp.any(ahead & (place[:, None] == place[None, :]), 0)
    source = shared_row(owner, col_index & 1, wide, narrow, BATCHES * CAP)
    source = source + batch * CAP + second.astype(jnp.int32)
    px = owner // narrow * tile_x + cell // tile_y - row_index * tile_x
    py = owner % narrow * tile_y + cell % tile_y - col_index * tile_y
    pick = (position[None, :] == order[:, None]).astype(jnp.float32)
    table = jnp.stack(
        [
            source.astype(jnp.float32),
            place.astype(jnp.float32),
            px.astype(jnp.float32),
            py.astype(jnp.float32),
            value,
            var,
        ],
        0,
    )
    table = lax.dot_general(
        table, pick, (((1,), (1,)), ((), ())), precision=lax.Precision.HIGHEST
    )
    source = (table[0] + 0.5).astype(jnp.int32)
    place = table[1]
    edge = jnp.full((1,), -1.0, jnp.float32)
    follows = (place == jnp.concatenate([edge, place[:-1]])).astype(jnp.float32)
    leads = (place == jnp.concatenate([place[1:], edge])).astype(jnp.float32)

    def mate(row):
        zero = jnp.zeros((1,), jnp.float32)
        return leads * jnp.concatenate([row[1:], zero]) + follows * jnp.concatenate(
            [zero, row[:-1]]
        )

    rows = jnp.stack(
        [
            table[4],
            table[5],
            mate(table[4]),
            mate(table[5]) + (1.0 - leads - follows),
            leads,
            follows,
            table[2],
            table[3],
        ],
        0,
    )
    return source, rows


def split(value):
    high = value.astype(jnp.bfloat16)
    low = (value - high.astype(jnp.float32)).astype(jnp.bfloat16)
    return high, low


def assimilate_kernel(
    tile_x,
    tile_y,
    reach_x,
    reach_y,
    source_ref,
    rows_ref,
    cols_ref,
    near_ref,
    far_ref,
    field_ref,
    out_ref,
    shared_ref,
    obs_ref,
    gain_a,
    gain_b,
    change_a,
    change_b,
    taper_x,
    taper_y,
):
    count, members = obs_ref.shape
    half = count // BATCHES
    scale_x = -0.5 / (reach_x * reach_x)
    scale_y = -0.5 / (reach_y * reach_y)

    near = near_ref.shape[0]
    shared_ref[:near, :] = near_ref[...]
    shared_ref[near:, :] = far_ref[...]

    def fetch(index, carry):
        obs_ref[pl.ds(index, 1), :] = shared_ref[pl.ds(source_ref[index], 1), :]
        return carry

    lax.fori_loop(0, count, fetch, 0, unroll=8)

    def prepare(batch):
        low = batch * half
        prior = obs_ref[low : low + half, :]
        cols = cols_ref[low : low + half, :]
        value, var, mate_value, mate_var = (cols[:, i : i + 1] for i in range(4))
        leads, follows = cols[:, 4:5], cols[:, 5:6]
        mean = jnp.mean(prior, 1, keepdims=True)
        own = prior - mean
        after = pltpu.roll(prior, half - 1, 0)
        before = pltpu.roll(prior, 1, 0)
        mate_prior = jnp.where(leads > 0.0, after, before)
        mate_mean = jnp.mean(mate_prior, 1, keepdims=True)
        paired = leads + follows
        mate = (mate_prior - mate_mean) * paired
        own_own = jnp.sum(own * own, 1, keepdims=True)
        own_mate = jnp.sum(own * mate, 1, keepdims=True)
        rest = mate - own * (own_mate / jnp.maximum(own_own, 1e-30))
        area = own_own * jnp.sum(rest * rest, 1, keepdims=True)
        mate_mate = jnp.sum(mate * mate, 1, keepdims=True)
        floor = jnp.float32(members - 1)
        own_floor, mate_floor = floor * var, floor * mate_var
        det = own_floor * mate_floor + own_floor * mate_mate + mate_floor * own_own + area
        own_part = (mate_floor * own_own + area) / det
        mate_part = own_floor * own_mate / det
        shift = own_part * (value - mean) + mate_part * paired * (mate_value - mate_mean)
        change = shift - 0.5 * (own_part * own + mate_part * mate)
        gain = (own / (own_own + EPS)).T
        high, low_part = split(gain)
        gain_a[:members, :] = high
        gain_a[members:, :] = high
        gain_b[...] = low_part
        high, low_part = split(change)
        change_a[:, :members] = high
        change_a[:, members:] = low_part
        change_b[...] = high

    def increment(cells, taper):
        anomaly = cells - jnp.mean(cells, 1, keepdims=True)
        high, low = split(anomaly)
        covary = jnp.dot(
            jnp.concatenate([high, low], 1), gain_a[...], preferred_element_type=jnp.float32
        ) + jnp.dot(high, gain_b[...], preferred_element_type=jnp.float32)
        high, low = split(covary * taper)
        both = jnp.dot(high, change_a[...], preferred_element_type=jnp.float32)
        rest = jnp.dot(low, change_b[...], preferred_element_type=jnp.float32)
        return cells + (both[:, :members] + both[:, members:] + rest)

    def update_field(batch, from_ref):
        low = batch * half
        obs_x = rows_ref[6:7, low : low + half]
        obs_y = rows_ref[7:8, low : low + half]
        at_x = lax.broadcasted_iota(jnp.int32, (tile_x, half), 0).astype(jnp.float32) - obs_x
        at_y = lax.broadcasted_iota(jnp.int32, (tile_y, half), 0).astype(jnp.float32) - obs_y
        taper_x[...] = jnp.exp(scale_x * (at_x * at_x))
        taper_y[...] = jnp.exp(scale_y * (at_y * at_y))

        for first in range(0, tile_x, GROUP):
            where = slice(first * tile_y, (first + GROUP) * tile_y)
            taper = jnp.concatenate(
                [taper_x[first + i : first + i + 1, :] * taper_y[...] for i in range(GROUP)], 0
            )
            out_ref[where, :] = increment(from_ref[where, :], taper)

    prepare(0)
    update_field(0, field_ref)
    chunk = min(half, 256)
    for start in range(half, count, chunk):
        gap_x = cols_ref[start : start + chunk, 6:7] - rows_ref[6:7, :half]
        gap_y = cols_ref[start : start + chunk, 7:8] - rows_ref[7:8, :half]
        taper = jnp.exp(scale_x * (gap_x * gap_x) + scale_y * (gap_y * gap_y))
        obs_ref[start : start + chunk, :] = increment(obs_ref[start : start + chunk, :], taper)
    prepare(1)
    update_field(1, out_ref)


def assimilate(source, rows, cols, near, far, field, tile_x, tile_y, reach_x, reach_y):
    cells, members = field.shape
    count = source.shape[0]
    half = count // BATCHES
    return pl.pallas_call(
        functools.partial(assimilate_kernel, tile_x, tile_y, reach_x, reach_y),
        name="assimilate",
        out_shape=jax.ShapeDtypeStruct((cells, members), jnp.float32),
        in_specs=[in_smem()] + [in_vmem()] * 5,
        out_specs=in_vmem(),
        scratch_shapes=[
            pltpu.VMEM((near.shape[0] + far.shape[0], members), jnp.float32),
            pltpu.VMEM((count, members), jnp.float32),
            pltpu.VMEM((2 * members, half), jnp.bfloat16),
            pltpu.VMEM((members, half), jnp.bfloat16),
            pltpu.VMEM((half, 2 * members), jnp.bfloat16),
            pltpu.VMEM((half, members), jnp.bfloat16),
            pltpu.VMEM((tile_x, half), jnp.float32),
            pltpu.VMEM((tile_y, half), jnp.float32),
        ],
        compiler_params=grant(40),
    )(source, rows, cols, near, far, field)


def per_device(ensemble, coefficients, obs_owner, obs_cell, obs_batch, obs_value, obs_var):
    wide = lax.axis_size("gx")
    narrow = lax.axis_size("gy")
    row_index = lax.axis_index("gx")
    col_index = lax.axis_index("gy")
    tile_x, tile_y, members = ensemble.shape
    reach_x = tile_x * wide / 2.0
    reach_y = tile_y * narrow / 2.0
    cells = local_cells(row_index * narrow + col_index, obs_owner, obs_cell, obs_batch)
    first, last = pack_x(ensemble, coefficients)
    before, after = exchange(last, first, "gx")
    first, last = pack_y(ensemble, coefficients, before, after)
    left, right = exchange(last, first, "gy")
    padded, columns, priors = look(
        wide, cells, ensemble, coefficients, before, after, left, right
    )
    priors, obs_owner, obs_cell, obs_batch = lax.optimization_barrier(
        (priors, obs_owner, obs_cell, obs_batch)
    )
    source, rows = arrange(
        row_index,
        col_index,
        tile_x,
        tile_y,
        wide,
        narrow,
        obs_owner,
        obs_cell,
        obs_batch,
        obs_value,
        obs_var,
    )
    near, far = share_all(priors)
    field = forecast(coefficients.shape[0], padded, columns)
    field = assimilate(
        source, rows, rows.T, near, far, field, tile_x, tile_y, reach_x, reach_y
    )
    return field.reshape(tile_x, tile_y, members)


def solution(mesh):
    placed = (P("gx", "gy", None), P(None, "gx", "gy"), P(), P(), P(), P(), P())
    return jax.shard_map(
        per_device, mesh=mesh, in_specs=placed, out_specs=P("gx", "gy", None), check_vma=False
    )
```

```python
import functools

import jax
import jax.numpy as jnp
from jax import lax
from jax.experimental import pallas as pl
from jax.experimental.pallas import tpu as pltpu
from jax.sharding import PartitionSpec as P

STEPS = 4
CAP = 2
GROUP = 12
BATCHES = 2
EPS = 1e-05
GY_FACTORS = {64: (8, 4, 2), 8: (2, 2, 2)}


def neighbours(axis):
    size = lax.axis_size(axis)
    up = [(i, i + 1) for i in range(size - 1)]
    return up, [(j, i) for i, j in up]


def exchange(to_next, to_previous, axis):
    up, down = neighbours(axis)
    return lax.ppermute(to_next, axis, up), lax.ppermute(to_previous, axis, down)


def in_vmem():
    return pl.BlockSpec(memory_space=pltpu.VMEM)


def in_smem():
    return pl.BlockSpec(memory_space=pltpu.SMEM)


def grant(mib):
    return pltpu.CompilerParams(vmem_limit_bytes=mib << 20)


LINES = 8
MARGIN = 8


def pack_x_kernel(field_ref, whole_ref, first_ref, last_ref, coefs_ref, sems):
    tile_x, tile_y, _ = field_ref.shape
    kinds = coefs_ref.shape[0]
    copies = [pltpu.make_async_copy(whole_ref, coefs_ref, sems.at[2])]
    for index, (out_ref, start) in enumerate(((first_ref, 0), (last_ref, tile_x - STEPS))):
        copies.append(
            pltpu.make_async_copy(
                field_ref.at[pl.ds(start, STEPS)], out_ref.at[:, pl.ds(0, tile_y)], sems.at[index]
            )
        )
    for copy in copies:
        copy.start()
    for out_ref in (first_ref, last_ref):
        out_ref[:, tile_y:, :] = jnp.zeros_like(out_ref[:, tile_y:, :])
    copies[0].wait()
    for out_ref, start in ((first_ref, 0), (last_ref, tile_x - STEPS)):
        for kind in range(kinds):
            part = coefs_ref[kind, start : start + STEPS, :]
            for i in range(STEPS):
                out_ref[i, tile_y + kind : tile_y + kind + 1, :tile_y] = part[i : i + 1, :]
    for copy in copies[1:]:
        copy.wait()


def pack_x(field, coefs):
    tile_x, tile_y, members = field.shape
    slab = jax.ShapeDtypeStruct((STEPS, tile_y + LINES, members), jnp.float32)
    return pl.pallas_call(
        pack_x_kernel,
        name="pack_x",
        out_shape=(slab, slab, jax.ShapeDtypeStruct(coefs.shape, jnp.float32)),
        in_specs=[pl.BlockSpec(memory_space=pl.ANY)] * 2,
        out_specs=(in_vmem(),) * 3,
        scratch_shapes=[pltpu.SemaphoreType.DMA((3,))],
        compiler_params=grant(4),
    )(*(pltpu.with_memory_space_constraint(a, pltpu.HBM) for a in (field, coefs)))


def pack_y_kernel(field_ref, coefs_ref, before_ref, after_ref, first_ref, last_ref):
    tile_x, tile_y, _ = field_ref.shape
    kinds = coefs_ref.shape[0]
    inner = slice(STEPS, STEPS + tile_x)
    outer = slice(STEPS + tile_x, 2 * STEPS + tile_x)
    for out_ref, start in ((first_ref, 0), (last_ref, tile_y - STEPS)):
        edge = slice(start, start + STEPS)
        out_ref[:STEPS, :STEPS, :] = before_ref[:, edge, :]
        out_ref[inner, :STEPS, :] = field_ref[:, edge, :]
        out_ref[outer, :STEPS, :] = after_ref[:, edge, :]
        out_ref[inner, STEPS:, :] = jnp.zeros_like(out_ref[inner, STEPS:, :])
        out_ref[:STEPS, STEPS:, :] = before_ref[:, tile_y : tile_y + LINES - STEPS, :]
        out_ref[outer, STEPS:, :] = after_ref[:, tile_y : tile_y + LINES - STEPS, :]
    for kind in range(kinds):
        part = coefs_ref[kind]
        for i in range(tile_x):
            for out_ref in (first_ref, last_ref):
                out_ref[STEPS + i, STEPS + kind : STEPS + kind + 1, :tile_y] = part[i : i + 1, :]


def pack_y(field, coefs, before, after):
    tile_x, tile_y, members = field.shape
    slab = jax.ShapeDtypeStruct((tile_x + 2 * STEPS, LINES, members), jnp.float32)
    return pl.pallas_call(
        pack_y_kernel,
        name="pack_y",
        out_shape=(slab, slab),
        in_specs=[in_vmem()] * 4,
        out_specs=(in_vmem(), in_vmem()),
        compiler_params=grant(8),
    )(field, coefs, before, after)


def advance(west, centre, east, diffuse, speed_x, speed_y):
    size = centre.shape[0]
    north = pltpu.roll(centre, size - 1, 0)
    south = pltpu.roll(centre, 1, 0)
    spread = east + west + north + south - 4.0 * centre
    carried = 0.5 * (speed_x * (east - west) + speed_y * (north - south))
    return centre + diffuse * spread - (1.0 + 0.5 * jnp.tanh(centre)) * carried


def look_kernel(
    copies,
    cells_ref,
    field_ref,
    coefs_ref,
    before_ref,
    after_ref,
    left_ref,
    right_ref,
    padded_ref,
    columns_ref,
    priors_ref,
    lines_ref,
    last_ref,
):
    tile_x, tile_y, members = field_ref.shape
    kinds = coefs_ref.shape[0]
    high_x, high_y = padded_ref.shape[0], padded_ref.shape[1]
    inner = slice(STEPS, STEPS + tile_x)
    outer = slice(STEPS + tile_x, high_x)
    own = slice(MARGIN, MARGIN + tile_y)
    padded_ref[:, :MARGIN, :] = jnp.zeros((high_x, MARGIN, members), jnp.float32)
    padded_ref[:, MARGIN + tile_y :, :] = jnp.zeros(
        (high_x, high_y - MARGIN - tile_y, members), jnp.float32
    )
    padded_ref[:STEPS, own, :] = before_ref[:, :tile_y, :]
    padded_ref[inner, own, :] = field_ref[...]
    padded_ref[outer, own, :] = after_ref[:, :tile_y, :]
    padded_ref[:, MARGIN - STEPS : MARGIN, :] = left_ref[:, :STEPS, :]
    padded_ref[:, MARGIN + tile_y : MARGIN + tile_y + STEPS, :] = right_ref[:, :STEPS, :]
    lane = lax.broadcasted_iota(jnp.int32, (high_x, members), 1)
    lines_ref[...] = jnp.zeros_like(lines_ref)
    for kind in range(kinds):
        base = kind * high_x
        lines_ref[base : base + STEPS, :] = before_ref[:, tile_y + kind, :]
        lines_ref[base + STEPS : base + STEPS + tile_x, :tile_y] = coefs_ref[kind]
        lines_ref[base + STEPS + tile_x : base + high_x, :] = after_ref[:, tile_y + kind, :]
        rows = slice(base, base + high_x)
        middle = pltpu.roll(lines_ref[rows, :], MARGIN, 1)
        left = pltpu.roll(left_ref[:, STEPS + kind, :], members + MARGIN - tile_y, 1)
        right = pltpu.roll(right_ref[:, STEPS + kind, :], MARGIN + tile_y, 1)
        line = jnp.where(lane < MARGIN, left, jnp.where(lane < MARGIN + tile_y, middle, right))
        near = (lane >= MARGIN - STEPS) & (lane < MARGIN + tile_y + STEPS)
        lines_ref[rows, :] = jnp.where(near, line, 0.0)
    columns_ref[...] = lines_ref[...].T
    width = 2 * STEPS + 1
    window = 24
    for slot in range(cells_ref.shape[0]):
        cell = cells_ref[slot]
        at_x = cell // tile_y
        at_y = cell % tile_y + (MARGIN - STEPS)
        start = pl.multiple_of(jnp.minimum(at_y // 8 * 8, high_y - window), 8)
        patch = [padded_ref[at_x + i, pl.ds(start, window), :] for i in range(width)]
        coefs = pltpu.roll(columns_ref[pl.ds(start, window), :], members - at_x, 1)
        for step in range(1, STEPS + 1):
            fresh = list(patch)
            for i in range(step, width - step):
                fresh[i] = advance(
                    patch[i - 1],
                    patch[i],
                    patch[i + 1],
                    *(coefs[:, k * high_x + i : k * high_x + i + 1] for k in range(kinds)),
                )
            patch = fresh
        last_ref[...] = patch[STEPS]
        prior = last_ref[pl.ds(at_y + STEPS - start, 1), :]
        for copy in range(copies):
            priors_ref[copy, slot : slot + 1, :] = prior


def look(copies, cells, field, coefs, before, after, left, right):
    tile_x, tile_y, members = field.shape
    high_x, high_y = tile_x + 2 * STEPS, tile_y + 2 * MARGIN
    return pl.pallas_call(
        functools.partial(look_kernel, copies),
        name="look",
        out_shape=(
            jax.ShapeDtypeStruct((high_x, high_y, members), jnp.float32),
            jax.ShapeDtypeStruct((members, members), jnp.float32),
            jax.ShapeDtypeStruct((copies, cells.shape[0], members), jnp.float32),
        ),
        in_specs=[in_smem()] + [in_vmem()] * 6,
        out_specs=(in_vmem(),) * 3,
        scratch_shapes=[
            pltpu.VMEM((members, members), jnp.float32),
            pltpu.VMEM((24, members), jnp.float32),
        ],
        compiler_params=grant(12),
    )(cells, field, coefs, before, after, left, right)


def forecast_kernel(kinds, padded_ref, columns_ref, out_ref, ping_ref, pong_ref, spread_ref):
    high_x, high_y, members = padded_ref.shape
    tile_x, tile_y = high_x - 2 * STEPS, high_y - 2 * MARGIN
    for index in range(kinds * high_x):
        spread_ref[index] = jnp.broadcast_to(
            columns_ref[:high_y, index : index + 1], (high_y, members)
        )
    source = padded_ref
    for step in range(1, STEPS + 1):
        final = step == STEPS
        target = (ping_ref, pong_ref)[step % 2]

        def one_row(x, carry):
            row = advance(
                source[x - 1],
                source[x],
                source[x + 1],
                *(spread_ref[kind * high_x + x] for kind in range(kinds)),
            )
            if final:
                where = pl.ds(pl.multiple_of((x - STEPS) * tile_y, tile_y), tile_y)
                out_ref[where, :] = row[MARGIN : MARGIN + tile_y]
            else:
                target[x] = row
            return carry

        lax.fori_loop(step, high_x - step, one_row, 0, unroll=2)
        source = target


def forecast(kinds, padded, columns):
    high_x, high_y, members = padded.shape
    tile_x, tile_y = high_x - 2 * STEPS, high_y - 2 * MARGIN
    work = STEPS * high_x * high_y * members
    return pl.pallas_call(
        functools.partial(forecast_kernel, kinds),
        name="forecast",
        out_shape=jax.ShapeDtypeStruct((tile_x * tile_y, members), jnp.float32),
        in_specs=[in_vmem()] * 2,
        out_specs=in_vmem(),
        scratch_shapes=[
            pltpu.VMEM((high_x, high_y, members), jnp.float32),
            pltpu.VMEM((high_x, high_y, members), jnp.float32),
            pltpu.VMEM((kinds * high_x, high_y, members), jnp.float32),
        ],
        compiler_params=grant(16),
        cost_estimate=pl.CostEstimate(
            flops=20 * work, bytes_accessed=8 * high_x * high_y * members, transcendentals=work
        ),
    )(padded, columns)


def share(rows, axis, count, groups=None):
    height, width = rows.shape
    copies = jnp.broadcast_to(rows[None], (count, height, width)).reshape(count * height, width)
    return lax.all_to_all(copies, axis, 0, 0, axis_index_groups=groups, tiled=True)


def share_all(copies, beside):
    ys, xs, cs = GY_FACTORS[lax.axis_size("gy")]

    def at(y, x, c):
        return (y * xs + x) * cs + c

    planes = [
        [z * ys * xs * cs + at(y, x, c) for y in range(ys) for z in range(lax.axis_size("gx"))]
        for x in range(xs)
        for c in range(cs)
    ]
    along_x = [[at(y, x, c) for x in range(xs)] for y in range(ys) for c in range(cs)]
    across = [(i, i ^ 1) for i in range(ys * xs * cs)]
    rows = lax.all_to_all(copies, ("gx", "gy"), 0, 0, axis_index_groups=planes, tiled=True)
    rows, beside = lax.optimization_barrier((rows.reshape(-1, rows.shape[-1]), beside))
    rows = share(rows, "gy", xs, along_x)
    return rows, lax.ppermute(rows, "gy", across), beside


def shared_row(owner, side, wide, narrow, slots):
    ys, xs, cs = GY_FACTORS[narrow]
    row, col = owner // narrow, owner % narrow
    y, x, c = col // (xs * cs), col // cs % xs, col % cs
    return ((((c ^ side) * xs + x) * ys + y) * wide + row) * slots


def local_cells(tile_id, obs_owner, obs_cell, obs_batch):
    span = 2048
    order = jnp.arange(obs_owner.shape[0], dtype=jnp.int32)
    key = (order * span + obs_cell)[None, :]
    batches = jnp.arange(BATCHES, dtype=jnp.int32)[:, None]
    mine = (obs_owner == tile_id)[None, :] & (obs_batch[None, :] == batches)
    first = jnp.min(jnp.where(mine, key, obs_owner.shape[0] * span), 1)
    last = jnp.max(jnp.where(mine, key, 0), 1)
    return jnp.stack([first, last], 1).reshape(-1) & (span - 1)


def sort(wide, narrow, owner, batch):
    count = owner.shape[0]
    order = jnp.arange(count, dtype=jnp.int32)
    place = batch * (wide * narrow) + owner
    key = place * count + order
    ahead = key[:, None] < key[None, :]
    position = jnp.sum(ahead.astype(jnp.int32), 0)
    second = jnp.sum((ahead & (place[:, None] == place[None, :])).astype(jnp.int32), 0)
    return position, second


def arrange(
    row_index, col_index, tile_x, tile_y, wide, narrow, owner, cell, batch, value, var, position, second
):
    count = owner.shape[0]
    order = jnp.arange(count, dtype=jnp.int32)
    place = batch * (wide * narrow) + owner
    source = shared_row(owner, col_index & 1, wide, narrow, BATCHES * CAP)
    source = source + batch * CAP + second
    px = owner // narrow * tile_x + cell // tile_y - row_index * tile_x
    py = owner % narrow * tile_y + cell % tile_y - col_index * tile_y
    pick = (position[None, :] == order[:, None]).astype(jnp.float32)
    table = jnp.stack(
        [
            source.astype(jnp.float32),
            place.astype(jnp.float32),
            px.astype(jnp.float32),
            py.astype(jnp.float32),
            value,
            var,
        ],
        0,
    )
    table = lax.dot_general(
        table, pick, (((1,), (1,)), ((), ())), precision=lax.Precision.HIGHEST
    )
    source = (table[0] + 0.5).astype(jnp.int32)
    place = table[1]
    edge = jnp.full((1,), -1.0, jnp.float32)
    follows = (place == jnp.concatenate([edge, place[:-1]])).astype(jnp.float32)
    leads = (place == jnp.concatenate([place[1:], edge])).astype(jnp.float32)

    def mate(row):
        zero = jnp.zeros((1,), jnp.float32)
        return leads * jnp.concatenate([row[1:], zero]) + follows * jnp.concatenate(
            [zero, row[:-1]]
        )

    rows = jnp.stack(
        [
            table[4],
            table[5],
            mate(table[4]),
            mate(table[5]) + (1.0 - leads - follows),
            leads,
            follows,
            table[2],
            table[3],
        ],
        0,
    )
    return source, rows


def split(value):
    high = value.astype(jnp.bfloat16)
    low = (value - high.astype(jnp.float32)).astype(jnp.bfloat16)
    return high, low


def assimilate_kernel(
    tile_x,
    tile_y,
    reach_x,
    reach_y,
    source_ref,
    rows_ref,
    cols_ref,
    near_ref,
    far_ref,
    field_ref,
    out_ref,
    shared_ref,
    obs_ref,
    gain_a,
    gain_b,
    change_a,
    change_b,
    taper_x,
    taper_y,
):
    count, members = obs_ref.shape
    half = count // BATCHES
    scale_x = -0.5 / (reach_x * reach_x)
    scale_y = -0.5 / (reach_y * reach_y)

    near = near_ref.shape[0]
    shared_ref[:near, :] = near_ref[...]
    shared_ref[near:, :] = far_ref[...]

    def fetch(index, carry):
        obs_ref[pl.ds(index, 1), :] = shared_ref[pl.ds(source_ref[index], 1), :]
        return carry

    lax.fori_loop(0, count, fetch, 0, unroll=8)

    def prepare(batch):
        low = batch * half
        prior = obs_ref[low : low + half, :]
        cols = cols_ref[low : low + half, :]
        value, var, mate_value, mate_var = (cols[:, i : i + 1] for i in range(4))
        leads, follows = cols[:, 4:5], cols[:, 5:6]
        mean = jnp.mean(prior, 1, keepdims=True)
        own = prior - mean
        after = pltpu.roll(prior, half - 1, 0)
        before = pltpu.roll(prior, 1, 0)
        mate_prior = jnp.where(leads > 0.0, after, before)
        mate_mean = jnp.mean(mate_prior, 1, keepdims=True)
        paired = leads + follows
        mate = (mate_prior - mate_mean) * paired
        own_own = jnp.sum(own * own, 1, keepdims=True)
        own_mate = jnp.sum(own * mate, 1, keepdims=True)
        rest = mate - own * (own_mate / jnp.maximum(own_own, 1e-30))
        area = own_own * jnp.sum(rest * rest, 1, keepdims=True)
        mate_mate = jnp.sum(mate * mate, 1, keepdims=True)
        floor = jnp.float32(members - 1)
        own_floor, mate_floor = floor * var, floor * mate_var
        det = own_floor * mate_floor + own_floor * mate_mate + mate_floor * own_own + area
        own_part = (mate_floor * own_own + area) / det
        mate_part = own_floor * own_mate / det
        shift = own_part * (value - mean) + mate_part * paired * (mate_value - mate_mean)
        change = shift - 0.5 * (own_part * own + mate_part * mate)
        gain = (own / (own_own + EPS)).T
        high, low_part = split(gain)
        gain_a[batch, :members, :] = high
        gain_a[batch, members:, :] = high
        gain_b[batch] = low_part
        high, low_part = split(change)
        change_a[batch, :, :members] = high
        change_a[batch, :, members:] = low_part
        change_b[batch] = high

    def increment(batch, cells, taper):
        anomaly = cells - jnp.mean(cells, 1, keepdims=True)
        high, low = split(anomaly)
        covary = jnp.dot(
            jnp.concatenate([high, low], 1), gain_a[batch], preferred_element_type=jnp.float32
        ) + jnp.dot(high, gain_b[batch], preferred_element_type=jnp.float32)
        high, low = split(covary * taper)
        both = jnp.dot(high, change_a[batch], preferred_element_type=jnp.float32)
        rest = jnp.dot(low, change_b[batch], preferred_element_type=jnp.float32)
        return cells + (both[:, :members] + both[:, members:] + rest)

    def update_field(batch, from_ref):
        low = batch * half
        obs_x = rows_ref[6:7, low : low + half]
        obs_y = rows_ref[7:8, low : low + half]
        at_x = lax.broadcasted_iota(jnp.int32, (tile_x, half), 0).astype(jnp.float32) - obs_x
        at_y = lax.broadcasted_iota(jnp.int32, (tile_y, half), 0).astype(jnp.float32) - obs_y
        taper_x[...] = jnp.exp(scale_x * (at_x * at_x))
        taper_y[...] = jnp.exp(scale_y * (at_y * at_y))

        for first in range(0, tile_x, GROUP):
            where = slice(first * tile_y, (first + GROUP) * tile_y)
            taper = jnp.concatenate(
                [taper_x[first + i : first + i + 1, :] * taper_y[...] for i in range(GROUP)], 0
            )
            out_ref[where, :] = increment(batch, from_ref[where, :], taper)

    prepare(0)
    chunk = min(half, 256)
    for start in range(half, count, chunk):
        gap_x = cols_ref[start : start + chunk, 6:7] - rows_ref[6:7, :half]
        gap_y = cols_ref[start : start + chunk, 7:8] - rows_ref[7:8, :half]
        taper = jnp.exp(scale_x * (gap_x * gap_x) + scale_y * (gap_y * gap_y))
        obs_ref[start : start + chunk, :] = increment(0, obs_ref[start : start + chunk, :], taper)
    prepare(1)
    update_field(0, field_ref)
    update_field(1, out_ref)


def assimilate(source, rows, cols, near, far, field, tile_x, tile_y, reach_x, reach_y):
    cells, members = field.shape
    count = source.shape[0]
    half = count // BATCHES
    return pl.pallas_call(
        functools.partial(assimilate_kernel, tile_x, tile_y, reach_x, reach_y),
        name="assimilate",
        out_shape=jax.ShapeDtypeStruct((cells, members), jnp.float32),
        in_specs=[in_smem()] + [in_vmem()] * 5,
        out_specs=in_vmem(),
        scratch_shapes=[
            pltpu.VMEM((near.shape[0] + far.shape[0], members), jnp.float32),
            pltpu.VMEM((count, members), jnp.float32),
            pltpu.VMEM((BATCHES, 2 * members, half), jnp.bfloat16),
            pltpu.VMEM((BATCHES, members, half), jnp.bfloat16),
            pltpu.VMEM((BATCHES, half, 2 * members), jnp.bfloat16),
            pltpu.VMEM((BATCHES, half, members), jnp.bfloat16),
            pltpu.VMEM((tile_x, half), jnp.float32),
            pltpu.VMEM((tile_y, half), jnp.float32),
        ],
        compiler_params=grant(40),
    )(source, rows, cols, near, far, field)


def per_device(ensemble, coefficients, obs_owner, obs_cell, obs_batch, obs_value, obs_var):
    wide = lax.axis_size("gx")
    narrow = lax.axis_size("gy")
    row_index = lax.axis_index("gx")
    col_index = lax.axis_index("gy")
    tile_x, tile_y, members = ensemble.shape
    reach_x = tile_x * wide / 2.0
    reach_y = tile_y * narrow / 2.0
    cells = local_cells(row_index * narrow + col_index, obs_owner, obs_cell, obs_batch)
    position, second = sort(wide, narrow, obs_owner, obs_batch)
    first, last, coefs = pack_x(ensemble, coefficients)
    before, after = exchange(last, first, "gx")
    first, last = pack_y(ensemble, coefs, before, after)
    left, right = exchange(last, first, "gy")
    padded, columns, priors = look(
        wide * GY_FACTORS[narrow][0], cells, ensemble, coefs, before, after, left, right
    )
    priors, position, second = lax.optimization_barrier((priors, position, second))
    source, rows = arrange(
        row_index,
        col_index,
        tile_x,
        tile_y,
        wide,
        narrow,
        obs_owner,
        obs_cell,
        obs_batch,
        obs_value,
        obs_var,
        position,
        second,
    )
    field = forecast(coefficients.shape[0], padded, columns)
    near, far, (field, source, rows, cols) = share_all(priors, (field, source, rows, rows.T))
    field = assimilate(
        source, rows, cols, near, far, field, tile_x, tile_y, reach_x, reach_y
    )
    return field.reshape(tile_x, tile_y, members)


def solution(mesh):
    placed = (P("gx", "gy", None), P(None, "gx", "gy"), P(), P(), P(), P(), P())
    return jax.shard_map(
        per_device, mesh=mesh, in_specs=placed, out_specs=P("gx", "gy", None), check_vma=False
    )
```

```python
import functools

import jax
import jax.numpy as jnp
from jax import lax
from jax.experimental import pallas as pl
from jax.experimental.pallas import tpu as pltpu
from jax.sharding import PartitionSpec as P

STEPS = 4
CAP = 2
GROUP = 12
BATCHES = 2
EPS = 1e-05
GY_FACTORS = {64: (8, 4, 2), 8: (2, 2, 2)}


def neighbours(axis):
    size = lax.axis_size(axis)
    up = [(i, i + 1) for i in range(size - 1)]
    return up, [(j, i) for i, j in up]


def exchange(to_next, to_previous, axis):
    up, down = neighbours(axis)
    return lax.ppermute(to_next, axis, up), lax.ppermute(to_previous, axis, down)


def in_vmem():
    return pl.BlockSpec(memory_space=pltpu.VMEM)


def in_smem():
    return pl.BlockSpec(memory_space=pltpu.SMEM)


def grant(mib):
    return pltpu.CompilerParams(vmem_limit_bytes=mib << 20)


LINES = 8
MARGIN = 8


def pack_x_kernel(field_ref, whole_ref, first_ref, last_ref, coefs_ref, sems):
    tile_x, tile_y, _ = field_ref.shape
    kinds = coefs_ref.shape[0]
    copies = [pltpu.make_async_copy(whole_ref, coefs_ref, sems.at[2])]
    for index, (out_ref, start) in enumerate(((first_ref, 0), (last_ref, tile_x - STEPS))):
        copies.append(
            pltpu.make_async_copy(
                field_ref.at[pl.ds(start, STEPS)], out_ref.at[:, pl.ds(0, tile_y)], sems.at[index]
            )
        )
    for copy in copies:
        copy.start()
    for out_ref in (first_ref, last_ref):
        out_ref[:, tile_y:, :] = jnp.zeros_like(out_ref[:, tile_y:, :])
    copies[0].wait()
    for out_ref, start in ((first_ref, 0), (last_ref, tile_x - STEPS)):
        for kind in range(kinds):
            part = coefs_ref[kind, start : start + STEPS, :]
            for i in range(STEPS):
                out_ref[i, tile_y + kind : tile_y + kind + 1, :tile_y] = part[i : i + 1, :]
    for copy in copies[1:]:
        copy.wait()


def pack_x(field, coefs):
    _, tile_y, members = field.shape
    slab = jax.ShapeDtypeStruct((STEPS, tile_y + LINES, members), jnp.float32)
    return pl.pallas_call(
        pack_x_kernel,
        name="pack_x",
        out_shape=(slab, slab, jax.ShapeDtypeStruct(coefs.shape, jnp.float32)),
        in_specs=[pl.BlockSpec(memory_space=pl.ANY)] * 2,
        out_specs=(in_vmem(),) * 3,
        scratch_shapes=[pltpu.SemaphoreType.DMA((3,))],
        compiler_params=grant(4),
    )(*(pltpu.with_memory_space_constraint(a, pltpu.HBM) for a in (field, coefs)))


def pack_y_kernel(field_ref, coefs_ref, before_ref, after_ref, first_ref, last_ref):
    tile_x, tile_y, _ = field_ref.shape
    kinds = coefs_ref.shape[0]
    inner = slice(STEPS, STEPS + tile_x)
    outer = slice(STEPS + tile_x, 2 * STEPS + tile_x)
    for out_ref, start in ((first_ref, 0), (last_ref, tile_y - STEPS)):
        edge = slice(start, start + STEPS)
        out_ref[:STEPS, :STEPS, :] = before_ref[:, edge, :]
        out_ref[inner, :STEPS, :] = field_ref[:, edge, :]
        out_ref[outer, :STEPS, :] = after_ref[:, edge, :]
        out_ref[inner, STEPS:, :] = jnp.zeros_like(out_ref[inner, STEPS:, :])
        out_ref[:STEPS, STEPS:, :] = before_ref[:, tile_y : tile_y + LINES - STEPS, :]
        out_ref[outer, STEPS:, :] = after_ref[:, tile_y : tile_y + LINES - STEPS, :]
    for kind in range(kinds):
        part = coefs_ref[kind]
        for i in range(tile_x):
            for out_ref in (first_ref, last_ref):
                out_ref[STEPS + i, STEPS + kind : STEPS + kind + 1, :tile_y] = part[i : i + 1, :]


def pack_y(field, coefs, before, after):
    tile_x, _, members = field.shape
    slab = jax.ShapeDtypeStruct((tile_x + 2 * STEPS, LINES, members), jnp.float32)
    return pl.pallas_call(
        pack_y_kernel,
        name="pack_y",
        out_shape=(slab, slab),
        in_specs=[in_vmem()] * 4,
        out_specs=(in_vmem(), in_vmem()),
        compiler_params=grant(8),
    )(field, coefs, before, after)


def advance(west, centre, east, diffuse, speed_x, speed_y):
    size = centre.shape[0]
    north = pltpu.roll(centre, size - 1, 0)
    south = pltpu.roll(centre, 1, 0)
    spread = east + west + north + south - 4.0 * centre
    carried = 0.5 * (speed_x * (east - west) + speed_y * (north - south))
    return centre + diffuse * spread - (1.0 + 0.5 * jnp.tanh(centre)) * carried


def look_kernel(
    copies,
    cells_ref,
    field_ref,
    coefs_ref,
    before_ref,
    after_ref,
    left_ref,
    right_ref,
    padded_ref,
    columns_ref,
    priors_ref,
    lines_ref,
    last_ref,
):
    tile_x, tile_y, members = field_ref.shape
    kinds = coefs_ref.shape[0]
    high_x, high_y = padded_ref.shape[0], padded_ref.shape[1]
    inner = slice(STEPS, STEPS + tile_x)
    outer = slice(STEPS + tile_x, high_x)
    own = slice(MARGIN, MARGIN + tile_y)
    padded_ref[:, :MARGIN, :] = jnp.zeros((high_x, MARGIN, members), jnp.float32)
    padded_ref[:, MARGIN + tile_y :, :] = jnp.zeros(
        (high_x, high_y - MARGIN - tile_y, members), jnp.float32
    )
    padded_ref[:STEPS, own, :] = before_ref[:, :tile_y, :]
    padded_ref[inner, own, :] = field_ref[...]
    padded_ref[outer, own, :] = after_ref[:, :tile_y, :]
    padded_ref[:, MARGIN - STEPS : MARGIN, :] = left_ref[:, :STEPS, :]
    padded_ref[:, MARGIN + tile_y : MARGIN + tile_y + STEPS, :] = right_ref[:, :STEPS, :]
    lane = lax.broadcasted_iota(jnp.int32, (high_x, members), 1)
    lines_ref[...] = jnp.zeros_like(lines_ref)
    for kind in range(kinds):
        base = kind * high_x
        lines_ref[base : base + STEPS, :] = before_ref[:, tile_y + kind, :]
        lines_ref[base + STEPS : base + STEPS + tile_x, :tile_y] = coefs_ref[kind]
        lines_ref[base + STEPS + tile_x : base + high_x, :] = after_ref[:, tile_y + kind, :]
        rows = slice(base, base + high_x)
        middle = pltpu.roll(lines_ref[rows, :], MARGIN, 1)
        left = pltpu.roll(left_ref[:, STEPS + kind, :], members + MARGIN - tile_y, 1)
        right = pltpu.roll(right_ref[:, STEPS + kind, :], MARGIN + tile_y, 1)
        line = jnp.where(lane < MARGIN, left, jnp.where(lane < MARGIN + tile_y, middle, right))
        near = (lane >= MARGIN - STEPS) & (lane < MARGIN + tile_y + STEPS)
        lines_ref[rows, :] = jnp.where(near, line, 0.0)
    columns_ref[...] = lines_ref[...].T
    width = 2 * STEPS + 1
    window = 24
    for slot in range(cells_ref.shape[0]):
        cell = cells_ref[slot]
        at_x = cell // tile_y
        at_y = cell % tile_y + (MARGIN - STEPS)
        start = pl.multiple_of(jnp.minimum(at_y // 8 * 8, high_y - window), 8)
        patch = [padded_ref[at_x + i, pl.ds(start, window), :] for i in range(width)]
        coefs = pltpu.roll(columns_ref[pl.ds(start, window), :], members - at_x, 1)
        for step in range(1, STEPS + 1):
            fresh = list(patch)
            for i in range(step, width - step):
                fresh[i] = advance(
                    patch[i - 1],
                    patch[i],
                    patch[i + 1],
                    *(coefs[:, k * high_x + i : k * high_x + i + 1] for k in range(kinds)),
                )
            patch = fresh
        last_ref[...] = patch[STEPS]
        prior = last_ref[pl.ds(at_y + STEPS - start, 1), :]
        for copy in range(copies):
            priors_ref[copy, slot : slot + 1, :] = prior


def look(copies, cells, field, coefs, before, after, left, right):
    tile_x, tile_y, members = field.shape
    high_x, high_y = tile_x + 2 * STEPS, tile_y + 2 * MARGIN
    return pl.pallas_call(
        functools.partial(look_kernel, copies),
        name="look",
        out_shape=(
            jax.ShapeDtypeStruct((high_x, high_y, members), jnp.float32),
            jax.ShapeDtypeStruct((members, members), jnp.float32),
            jax.ShapeDtypeStruct((copies, cells.shape[0], members), jnp.float32),
        ),
        in_specs=[in_smem()] + [in_vmem()] * 6,
        out_specs=(in_vmem(),) * 3,
        scratch_shapes=[
            pltpu.VMEM((members, members), jnp.float32),
            pltpu.VMEM((24, members), jnp.float32),
        ],
        compiler_params=grant(12),
    )(cells, field, coefs, before, after, left, right)


def forecast_kernel(kinds, padded_ref, columns_ref, out_ref, ping_ref, pong_ref, spread_ref):
    high_x, high_y, members = padded_ref.shape
    tile_y = high_y - 2 * MARGIN
    for index in range(kinds * high_x):
        spread_ref[index] = jnp.broadcast_to(
            columns_ref[:high_y, index : index + 1], (high_y, members)
        )
    source = padded_ref
    for step in range(1, STEPS + 1):
        final = step == STEPS
        target = (ping_ref, pong_ref)[step % 2]

        def one_row(x, carry):
            row = advance(
                source[x - 1],
                source[x],
                source[x + 1],
                *(spread_ref[kind * high_x + x] for kind in range(kinds)),
            )
            if final:
                where = pl.ds(pl.multiple_of((x - STEPS) * tile_y, tile_y), tile_y)
                out_ref[where, :] = row[MARGIN : MARGIN + tile_y]
            else:
                target[x] = row
            return carry

        lax.fori_loop(step, high_x - step, one_row, 0, unroll=2)
        source = target


def forecast(kinds, padded, columns):
    high_x, high_y, members = padded.shape
    tile_x, tile_y = high_x - 2 * STEPS, high_y - 2 * MARGIN
    work = STEPS * high_x * high_y * members
    return pl.pallas_call(
        functools.partial(forecast_kernel, kinds),
        name="forecast",
        out_shape=jax.ShapeDtypeStruct((tile_x * tile_y, members), jnp.float32),
        in_specs=[in_vmem()] * 2,
        out_specs=in_vmem(),
        scratch_shapes=[
            pltpu.VMEM((high_x, high_y, members), jnp.float32),
            pltpu.VMEM((high_x, high_y, members), jnp.float32),
            pltpu.VMEM((kinds * high_x, high_y, members), jnp.float32),
        ],
        compiler_params=grant(16),
        cost_estimate=pl.CostEstimate(
            flops=20 * work, bytes_accessed=8 * high_x * high_y * members, transcendentals=work
        ),
    )(padded, columns)


def share(rows, axis, count, groups=None):
    height, width = rows.shape
    copies = jnp.broadcast_to(rows[None], (count, height, width)).reshape(count * height, width)
    return lax.all_to_all(copies, axis, 0, 0, axis_index_groups=groups, tiled=True)


def along_planes(narrow, wide):
    ys, xs, cs = GY_FACTORS[narrow]

    def at(y, x, c):
        return (y * xs + x) * cs + c

    planes = [
        [z * narrow + at(y, x, c) for y in range(ys) for z in range(wide)]
        for x in range(xs)
        for c in range(cs)
    ]
    lines = [[at(y, x, c) for x in range(xs)] for y in range(ys) for c in range(cs)]
    across = [(i, i ^ 1) for i in range(narrow)]
    return planes, lines, across


def gather_kernel(rows_ref, rank_ref, first_ref, rest_ref):
    slots = rows_ref.shape[0]
    copies, room = first_ref.shape[0], first_ref.shape[1]
    rank = lax.broadcasted_iota(jnp.int32, (slots, slots), 0).astype(jnp.float32)
    pick = (rank == rank_ref[...]).astype(jnp.float32).astype(jnp.bfloat16)
    left = rows_ref[...]
    packed = jnp.zeros_like(left)
    for _ in range(3):
        part = left.astype(jnp.bfloat16)
        packed = packed + jnp.dot(pick, part, preferred_element_type=jnp.float32)
        left = left - part.astype(jnp.float32)
    for copy in range(copies):
        first_ref[copy] = packed[:room]
    rest_ref[...] = packed[room:]


def gather(rows, rank, copies, room):
    slots, members = rows.shape
    return pl.pallas_call(
        gather_kernel,
        name="gather",
        out_shape=(
            jax.ShapeDtypeStruct((copies, room, members), jnp.float32),
            jax.ShapeDtypeStruct((slots - room, members), jnp.float32),
        ),
        in_specs=[in_vmem()] * 2,
        out_specs=(in_vmem(),) * 2,
        compiler_params=grant(8),
    )(rows, rank)


def share_all(copies, rank, crowded, wide, narrow, beside):
    xs = GY_FACTORS[narrow][1]
    planes, lines, across = along_planes(narrow, wide)
    rows = lax.all_to_all(copies, ("gx", "gy"), 0, 0, axis_index_groups=planes, tiled=True)
    rows = rows.reshape(-1, rows.shape[-1])
    slots, members = rows.shape
    rows, rank, crowded, beside = lax.optimization_barrier((rows, rank, crowded, beside))
    first, rest = gather(rows, rank, xs, slots // 2)
    near = lax.all_to_all(first.reshape(-1, members), "gy", 0, 0, axis_index_groups=lines, tiled=True)
    far = lax.ppermute(near, "gy", across)

    def send(rest):
        near = share(rest, "gy", xs, lines)
        return near, lax.ppermute(near, "gy", across)

    def skip(rest):
        blank = jnp.zeros((xs * rest.shape[0], members), jnp.float32)
        return blank, blank

    more_near, more_far = lax.cond(crowded, send, skip, rest)
    return (near, far, more_near, more_far), beside


def local_cells(tile_id, obs_owner, obs_cell, obs_batch):
    span = 2048
    order = jnp.arange(obs_owner.shape[0], dtype=jnp.int32)
    key = (order * span + obs_cell)[None, :]
    batches = jnp.arange(BATCHES, dtype=jnp.int32)[:, None]
    mine = (obs_owner == tile_id)[None, :] & (obs_batch[None, :] == batches)
    first = jnp.min(jnp.where(mine, key, obs_owner.shape[0] * span), 1)
    last = jnp.max(jnp.where(mine, key, 0), 1)
    return jnp.stack([first, last], 1).reshape(-1) & (span - 1)


def locate(wide, narrow, owner):
    _, xs, cs = GY_FACTORS[narrow]
    row, col = owner // narrow, owner % narrow
    y, x, c = col // (xs * cs), col // cs % xs, col % cs
    return c * xs + x, y * wide + row


def sort(wide, narrow, owner, batch):
    count = owner.shape[0]
    ys, xs, cs = GY_FACTORS[narrow]
    plane, tile = locate(wide, narrow, owner)
    place = (batch * (xs * cs) + plane) * (ys * wide) + tile
    key = place * count + jnp.arange(count, dtype=jnp.int32)
    ahead = key[:, None] < key[None, :]
    position = jnp.sum(ahead.astype(jnp.int32), 0)
    second = jnp.sum((ahead & (place[:, None] == place[None, :])).astype(jnp.int32), 0)
    return position, second


def arrange(
    row_index, col_index, tile_x, tile_y, wide, narrow, owner, cell, batch, value, var, position, second
):
    count = owner.shape[0]
    ys, xs, cs = GY_FACTORS[narrow]
    number = xs * cs
    slots = ys * wide * BATCHES * CAP
    room = slots // 2
    side = col_index % cs
    own_plane = side * xs + col_index // cs % xs
    order = jnp.arange(count, dtype=jnp.int32)
    plane, tile = locate(wide, narrow, owner)
    group = batch * number + plane
    place = group * (ys * wide) + tile
    groups = jnp.arange(BATCHES * number, dtype=jnp.int32)
    member = (group[None, :] == groups[:, None]).astype(jnp.int32)
    held = jnp.sum(member, 1)
    before = jnp.sum(jnp.where(groups[None, :] < groups[:, None], held[None, :], 0), 1)
    base = jnp.concatenate([jnp.zeros((number,), jnp.int32), held[:number]])
    rank = position + jnp.sum(member * (base - before)[:, None], 0)
    crowded = jnp.any(held[:number] + held[number:] > room)
    slot = tile * (BATCHES * CAP) + batch * CAP + second
    here = (plane == own_plane)[None, :] & (
        slot[None, :] == jnp.arange(slots, dtype=jnp.int32)[:, None]
    )
    own_rank = (jnp.sum(jnp.where(here, rank[None, :] + 1, 0), 1) - 1).astype(jnp.float32)[None, :]
    shelf = ((plane // xs) ^ side) * xs + plane % xs
    source = jnp.where(
        rank < room,
        shelf * room + rank,
        number * room + shelf * (slots - room) + (rank - room),
    )
    px = owner // narrow * tile_x + cell // tile_y - row_index * tile_x
    py = owner % narrow * tile_y + cell % tile_y - col_index * tile_y
    pick = (position[None, :] == order[:, None]).astype(jnp.float32)
    table = jnp.stack(
        [
            source.astype(jnp.float32),
            place.astype(jnp.float32),
            px.astype(jnp.float32),
            py.astype(jnp.float32),
            value,
            var,
        ],
        0,
    )
    table = lax.dot_general(table, pick, (((1,), (1,)), ((), ())), precision=lax.Precision.HIGHEST)
    source = (table[0] + 0.5).astype(jnp.int32)
    place = table[1]
    edge = jnp.full((1,), -1.0, jnp.float32)
    follows = (place == jnp.concatenate([edge, place[:-1]])).astype(jnp.float32)
    leads = (place == jnp.concatenate([place[1:], edge])).astype(jnp.float32)

    def mate(row):
        zero = jnp.zeros((1,), jnp.float32)
        return leads * jnp.concatenate([row[1:], zero]) + follows * jnp.concatenate(
            [zero, row[:-1]]
        )

    rows = jnp.stack(
        [
            table[4],
            table[5],
            mate(table[4]),
            mate(table[5]) + (1.0 - leads - follows),
            leads,
            follows,
            table[2],
            table[3],
        ],
        0,
    )
    return source, rows, own_rank, crowded


def split(value):
    high = value.astype(jnp.bfloat16)
    low = (value - high.astype(jnp.float32)).astype(jnp.bfloat16)
    return high, low


def assimilate_kernel(
    tile_x,
    tile_y,
    reach_x,
    reach_y,
    source_ref,
    rows_ref,
    cols_ref,
    near_ref,
    far_ref,
    more_near_ref,
    more_far_ref,
    field_ref,
    out_ref,
    shared_ref,
    obs_ref,
    gain_a,
    gain_b,
    change_a,
    change_b,
    taper_x,
    taper_y,
):
    count, members = obs_ref.shape
    half = count // BATCHES
    scale_x = -0.5 / (reach_x * reach_x)
    scale_y = -0.5 / (reach_y * reach_y)

    start = 0
    for part_ref in (near_ref, far_ref, more_near_ref, more_far_ref):
        shared_ref[start : start + part_ref.shape[0], :] = part_ref[...]
        start += part_ref.shape[0]

    def fetch(index, carry):
        obs_ref[pl.ds(index, 1), :] = shared_ref[pl.ds(source_ref[index], 1), :]
        return carry

    lax.fori_loop(0, count, fetch, 0, unroll=8)

    def prepare(batch):
        low = batch * half
        prior = obs_ref[low : low + half, :]
        cols = cols_ref[low : low + half, :]
        value, var, mate_value, mate_var = (cols[:, i : i + 1] for i in range(4))
        leads, follows = cols[:, 4:5], cols[:, 5:6]
        mean = jnp.mean(prior, 1, keepdims=True)
        own = prior - mean
        after = pltpu.roll(prior, half - 1, 0)
        before = pltpu.roll(prior, 1, 0)
        mate_prior = jnp.where(leads > 0.0, after, before)
        mate_mean = jnp.mean(mate_prior, 1, keepdims=True)
        paired = leads + follows
        mate = (mate_prior - mate_mean) * paired
        own_own = jnp.sum(own * own, 1, keepdims=True)
        own_mate = jnp.sum(own * mate, 1, keepdims=True)
        rest = mate - own * (own_mate / jnp.maximum(own_own, 1e-30))
        area = own_own * jnp.sum(rest * rest, 1, keepdims=True)
        mate_mate = jnp.sum(mate * mate, 1, keepdims=True)
        floor = jnp.float32(members - 1)
        own_floor, mate_floor = floor * var, floor * mate_var
        det = own_floor * mate_floor + own_floor * mate_mate + mate_floor * own_own + area
        own_part = (mate_floor * own_own + area) / det
        mate_part = own_floor * own_mate / det
        shift = own_part * (value - mean) + mate_part * paired * (mate_value - mate_mean)
        change = shift - 0.5 * (own_part * own + mate_part * mate)
        gain = (own / (own_own + EPS)).T
        high, low_part = split(gain)
        gain_a[batch, :members, :] = high
        gain_a[batch, members:, :] = high
        gain_b[batch] = low_part
        high, low_part = split(change)
        change_a[batch, :, :members] = high
        change_a[batch, :, members:] = low_part
        change_b[batch] = high

    def increment(batch, cells, taper):
        anomaly = cells - jnp.mean(cells, 1, keepdims=True)
        high, low = split(anomaly)
        covary = jnp.dot(
            jnp.concatenate([high, low], 1), gain_a[batch], preferred_element_type=jnp.float32
        ) + jnp.dot(high, gain_b[batch], preferred_element_type=jnp.float32)
        high, low = split(covary * taper)
        both = jnp.dot(high, change_a[batch], preferred_element_type=jnp.float32)
        rest = jnp.dot(low, change_b[batch], preferred_element_type=jnp.float32)
        return cells + (both[:, :members] + both[:, members:] + rest)

    def update_field(batch, from_ref):
        low = batch * half
        obs_x = rows_ref[6:7, low : low + half]
        obs_y = rows_ref[7:8, low : low + half]
        at_x = lax.broadcasted_iota(jnp.int32, (tile_x, half), 0).astype(jnp.float32) - obs_x
        at_y = lax.broadcasted_iota(jnp.int32, (tile_y, half), 0).astype(jnp.float32) - obs_y
        taper_x[...] = jnp.exp(scale_x * (at_x * at_x))
        taper_y[...] = jnp.exp(scale_y * (at_y * at_y))

        for first in range(0, tile_x, GROUP):
            where = slice(first * tile_y, (first + GROUP) * tile_y)
            taper = jnp.concatenate(
                [taper_x[first + i : first + i + 1, :] * taper_y[...] for i in range(GROUP)], 0
            )
            out_ref[where, :] = increment(batch, from_ref[where, :], taper)

    prepare(0)
    chunk = min(half, 256)
    for start in range(half, count, chunk):
        gap_x = cols_ref[start : start + chunk, 6:7] - rows_ref[6:7, :half]
        gap_y = cols_ref[start : start + chunk, 7:8] - rows_ref[7:8, :half]
        taper = jnp.exp(scale_x * (gap_x * gap_x) + scale_y * (gap_y * gap_y))
        obs_ref[start : start + chunk, :] = increment(0, obs_ref[start : start + chunk, :], taper)
    prepare(1)
    update_field(0, field_ref)
    update_field(1, out_ref)


def assimilate(source, rows, cols, shared, field, tile_x, tile_y, reach_x, reach_y):
    cells, members = field.shape
    count = source.shape[0]
    half = count // BATCHES
    return pl.pallas_call(
        functools.partial(assimilate_kernel, tile_x, tile_y, reach_x, reach_y),
        name="assimilate",
        out_shape=jax.ShapeDtypeStruct((cells, members), jnp.float32),
        in_specs=[in_smem()] + [in_vmem()] * (3 + len(shared)),
        out_specs=in_vmem(),
        scratch_shapes=[
            pltpu.VMEM((sum(part.shape[0] for part in shared), members), jnp.float32),
            pltpu.VMEM((count, members), jnp.float32),
            pltpu.VMEM((BATCHES, 2 * members, half), jnp.bfloat16),
            pltpu.VMEM((BATCHES, members, half), jnp.bfloat16),
            pltpu.VMEM((BATCHES, half, 2 * members), jnp.bfloat16),
            pltpu.VMEM((BATCHES, half, members), jnp.bfloat16),
            pltpu.VMEM((tile_x, half), jnp.float32),
            pltpu.VMEM((tile_y, half), jnp.float32),
        ],
        compiler_params=grant(40),
    )(source, rows, cols, *shared, field)


def per_device(ensemble, coefficients, obs_owner, obs_cell, obs_batch, obs_value, obs_var):
    wide = lax.axis_size("gx")
    narrow = lax.axis_size("gy")
    row_index = lax.axis_index("gx")
    col_index = lax.axis_index("gy")
    tile_x, tile_y, members = ensemble.shape
    reach_x = tile_x * wide / 2.0
    reach_y = tile_y * narrow / 2.0
    cells = local_cells(row_index * narrow + col_index, obs_owner, obs_cell, obs_batch)
    position, second = sort(wide, narrow, obs_owner, obs_batch)
    first, last, coefs = pack_x(ensemble, coefficients)
    before, after = exchange(last, first, "gx")
    first, last = pack_y(ensemble, coefs, before, after)
    left, right = exchange(last, first, "gy")
    padded, columns, priors = look(
        wide * GY_FACTORS[narrow][0], cells, ensemble, coefs, before, after, left, right
    )
    priors, position, second = lax.optimization_barrier((priors, position, second))
    source, rows, rank, crowded = arrange(
        row_index,
        col_index,
        tile_x,
        tile_y,
        wide,
        narrow,
        obs_owner,
        obs_cell,
        obs_batch,
        obs_value,
        obs_var,
        position,
        second,
    )
    field = forecast(coefficients.shape[0], padded, columns)
    shared, (field, source, rows, cols) = share_all(
        priors, rank, crowded, wide, narrow, (field, source, rows, rows.T)
    )
    field = assimilate(
        source, rows, cols, shared, field, tile_x, tile_y, reach_x, reach_y
    )
    return field.reshape(tile_x, tile_y, members)


def solution(mesh):
    placed = (P("gx", "gy", None), P(None, "gx", "gy"), P(), P(), P(), P(), P())
    return jax.shard_map(
        per_device, mesh=mesh, in_specs=placed, out_specs=P("gx", "gy", None), check_vma=False
    )
```

```python
import functools

import jax
import jax.numpy as jnp
from jax import lax
from jax.experimental import pallas as pl
from jax.experimental.pallas import tpu as pltpu
from jax.sharding import PartitionSpec as P

STEPS = 4
CAP = 2
GROUP = 12
BATCHES = 2
EPS = 1e-05
GY_FACTORS = {64: (8, 4, 2), 8: (2, 2, 2)}


def neighbours(axis):
    size = lax.axis_size(axis)
    up = [(i, i + 1) for i in range(size - 1)]
    return up, [(j, i) for i, j in up]


def exchange(to_next, to_previous, axis):
    up, down = neighbours(axis)
    return lax.ppermute(to_next, axis, up), lax.ppermute(to_previous, axis, down)


def in_vmem():
    return pl.BlockSpec(memory_space=pltpu.VMEM)


def in_smem():
    return pl.BlockSpec(memory_space=pltpu.SMEM)


def grant(mib):
    return pltpu.CompilerParams(vmem_limit_bytes=mib << 20)


LINES = 8
MARGIN = 8


def pack_x_kernel(field_ref, whole_ref, first_ref, last_ref, coefs_ref, sems):
    tile_x, tile_y, _ = field_ref.shape
    kinds = coefs_ref.shape[0]
    copies = [pltpu.make_async_copy(whole_ref, coefs_ref, sems.at[2])]
    for index, (out_ref, start) in enumerate(((first_ref, 0), (last_ref, tile_x - STEPS))):
        copies.append(
            pltpu.make_async_copy(
                field_ref.at[pl.ds(start, STEPS)], out_ref.at[:, pl.ds(0, tile_y)], sems.at[index]
            )
        )
    for copy in copies:
        copy.start()
    for out_ref in (first_ref, last_ref):
        out_ref[:, tile_y:, :] = jnp.zeros_like(out_ref[:, tile_y:, :])
    copies[0].wait()
    for out_ref, start in ((first_ref, 0), (last_ref, tile_x - STEPS)):
        for kind in range(kinds):
            part = coefs_ref[kind, start : start + STEPS, :]
            for i in range(STEPS):
                out_ref[i, tile_y + kind : tile_y + kind + 1, :tile_y] = part[i : i + 1, :]
    for copy in copies[1:]:
        copy.wait()


def pack_x(field, coefs):
    _, tile_y, members = field.shape
    slab = jax.ShapeDtypeStruct((STEPS, tile_y + LINES, members), jnp.float32)
    return pl.pallas_call(
        pack_x_kernel,
        name="pack_x",
        out_shape=(slab, slab, jax.ShapeDtypeStruct(coefs.shape, jnp.float32)),
        in_specs=[pl.BlockSpec(memory_space=pl.ANY)] * 2,
        out_specs=(in_vmem(),) * 3,
        scratch_shapes=[pltpu.SemaphoreType.DMA((3,))],
        compiler_params=grant(4),
    )(*(pltpu.with_memory_space_constraint(a, pltpu.HBM) for a in (field, coefs)))


def pack_y_kernel(field_ref, coefs_ref, before_ref, after_ref, first_ref, last_ref):
    tile_x, tile_y, _ = field_ref.shape
    kinds = coefs_ref.shape[0]
    inner = slice(STEPS, STEPS + tile_x)
    outer = slice(STEPS + tile_x, 2 * STEPS + tile_x)
    for out_ref, start in ((first_ref, 0), (last_ref, tile_y - STEPS)):
        edge = slice(start, start + STEPS)
        out_ref[:STEPS, :STEPS, :] = before_ref[:, edge, :]
        out_ref[inner, :STEPS, :] = field_ref[:, edge, :]
        out_ref[outer, :STEPS, :] = after_ref[:, edge, :]
        out_ref[inner, STEPS:, :] = jnp.zeros_like(out_ref[inner, STEPS:, :])
        out_ref[:STEPS, STEPS:, :] = before_ref[:, tile_y : tile_y + LINES - STEPS, :]
        out_ref[outer, STEPS:, :] = after_ref[:, tile_y : tile_y + LINES - STEPS, :]
    for kind in range(kinds):
        part = coefs_ref[kind]
        for i in range(tile_x):
            for out_ref in (first_ref, last_ref):
                out_ref[STEPS + i, STEPS + kind : STEPS + kind + 1, :tile_y] = part[i : i + 1, :]


def pack_y(field, coefs, before, after):
    tile_x, _, members = field.shape
    slab = jax.ShapeDtypeStruct((tile_x + 2 * STEPS, LINES, members), jnp.float32)
    return pl.pallas_call(
        pack_y_kernel,
        name="pack_y",
        out_shape=(slab, slab),
        in_specs=[in_vmem()] * 4,
        out_specs=(in_vmem(), in_vmem()),
        compiler_params=grant(8),
    )(field, coefs, before, after)


def advance(west, centre, east, diffuse, speed_x, speed_y):
    size = centre.shape[0]
    north = pltpu.roll(centre, size - 1, 0)
    south = pltpu.roll(centre, 1, 0)
    spread = east + west + north + south - 4.0 * centre
    carried = 0.5 * (speed_x * (east - west) + speed_y * (north - south))
    return centre + diffuse * spread - (1.0 + 0.5 * jnp.tanh(centre)) * carried


def look_kernel(
    copies,
    cells_ref,
    field_ref,
    coefs_ref,
    before_ref,
    after_ref,
    left_ref,
    right_ref,
    padded_ref,
    columns_ref,
    priors_ref,
    lines_ref,
    last_ref,
    found_ref,
):
    tile_x, tile_y, members = field_ref.shape
    kinds = coefs_ref.shape[0]
    high_x, high_y = padded_ref.shape[0], padded_ref.shape[1]
    inner = slice(STEPS, STEPS + tile_x)
    outer = slice(STEPS + tile_x, high_x)
    own = slice(MARGIN, MARGIN + tile_y)
    padded_ref[:, :MARGIN, :] = jnp.zeros((high_x, MARGIN, members), jnp.float32)
    padded_ref[:, MARGIN + tile_y :, :] = jnp.zeros(
        (high_x, high_y - MARGIN - tile_y, members), jnp.float32
    )
    padded_ref[:STEPS, own, :] = before_ref[:, :tile_y, :]
    padded_ref[inner, own, :] = field_ref[...]
    padded_ref[outer, own, :] = after_ref[:, :tile_y, :]
    padded_ref[:, MARGIN - STEPS : MARGIN, :] = left_ref[:, :STEPS, :]
    padded_ref[:, MARGIN + tile_y : MARGIN + tile_y + STEPS, :] = right_ref[:, :STEPS, :]
    lane = lax.broadcasted_iota(jnp.int32, (high_x, members), 1)
    lines_ref[...] = jnp.zeros_like(lines_ref)
    for kind in range(kinds):
        base = kind * high_x
        lines_ref[base : base + STEPS, :] = before_ref[:, tile_y + kind, :]
        lines_ref[base + STEPS : base + STEPS + tile_x, :tile_y] = coefs_ref[kind]
        lines_ref[base + STEPS + tile_x : base + high_x, :] = after_ref[:, tile_y + kind, :]
        rows = slice(base, base + high_x)
        middle = pltpu.roll(lines_ref[rows, :], MARGIN, 1)
        left = pltpu.roll(left_ref[:, STEPS + kind, :], members + MARGIN - tile_y, 1)
        right = pltpu.roll(right_ref[:, STEPS + kind, :], MARGIN + tile_y, 1)
        line = jnp.where(lane < MARGIN, left, jnp.where(lane < MARGIN + tile_y, middle, right))
        near = (lane >= MARGIN - STEPS) & (lane < MARGIN + tile_y + STEPS)
        lines_ref[rows, :] = jnp.where(near, line, 0.0)
    columns_ref[...] = lines_ref[...].T
    width = 2 * STEPS + 1
    window = 24
    for slot in range(cells_ref.shape[0]):
        cell = cells_ref[slot]
        at_x = cell // tile_y
        at_y = cell % tile_y + (MARGIN - STEPS)
        start = pl.multiple_of(jnp.minimum(at_y // 8 * 8, high_y - window), 8)
        patch = [padded_ref[at_x + i, pl.ds(start, window), :] for i in range(width)]
        coefs = pltpu.roll(columns_ref[pl.ds(start, window), :], members - at_x, 1)
        for step in range(1, STEPS + 1):
            fresh = list(patch)
            for i in range(step, width - step):
                fresh[i] = advance(
                    patch[i - 1],
                    patch[i],
                    patch[i + 1],
                    *(coefs[:, k * high_x + i : k * high_x + i + 1] for k in range(kinds)),
                )
            patch = fresh
        last_ref[slot] = patch[STEPS]
        found_ref[slot : slot + 1, :] = last_ref[slot, pl.ds(at_y + STEPS - start, 1), :]
    found = found_ref[: cells_ref.shape[0], :]
    for copy in range(copies):
        priors_ref[copy] = found


def look(copies, cells, field, coefs, before, after, left, right):
    tile_x, tile_y, members = field.shape
    high_x, high_y = tile_x + 2 * STEPS, tile_y + 2 * MARGIN
    return pl.pallas_call(
        functools.partial(look_kernel, copies),
        name="look",
        out_shape=(
            jax.ShapeDtypeStruct((high_x, high_y, members), jnp.float32),
            jax.ShapeDtypeStruct((members, members), jnp.float32),
            jax.ShapeDtypeStruct((copies, cells.shape[0], members), jnp.float32),
        ),
        in_specs=[in_smem()] + [in_vmem()] * 6,
        out_specs=(in_vmem(),) * 3,
        scratch_shapes=[
            pltpu.VMEM((members, members), jnp.float32),
            pltpu.VMEM((cells.shape[0], 24, members), jnp.float32),
            pltpu.VMEM((8, members), jnp.float32),
        ],
        compiler_params=grant(12),
    )(cells, field, coefs, before, after, left, right)


def forecast_kernel(kinds, padded_ref, columns_ref, out_ref, ping_ref, pong_ref, spread_ref):
    high_x, high_y, members = padded_ref.shape
    tile_y = high_y - 2 * MARGIN
    for index in range(kinds * high_x):
        spread_ref[index] = jnp.broadcast_to(
            columns_ref[:high_y, index : index + 1], (high_y, members)
        )
    source = padded_ref
    for step in range(1, STEPS + 1):
        final = step == STEPS
        target = (ping_ref, pong_ref)[step % 2]

        def one_row(x, carry):
            row = advance(
                source[x - 1],
                source[x],
                source[x + 1],
                *(spread_ref[kind * high_x + x] for kind in range(kinds)),
            )
            if final:
                where = pl.ds(pl.multiple_of((x - STEPS) * tile_y, tile_y), tile_y)
                out_ref[where, :] = row[MARGIN : MARGIN + tile_y]
            else:
                target[x] = row
            return carry

        lax.fori_loop(step, high_x - step, one_row, 0, unroll=2)
        source = target


def forecast(kinds, padded, columns):
    high_x, high_y, members = padded.shape
    tile_x, tile_y = high_x - 2 * STEPS, high_y - 2 * MARGIN
    work = STEPS * high_x * high_y * members
    return pl.pallas_call(
        functools.partial(forecast_kernel, kinds),
        name="forecast",
        out_shape=jax.ShapeDtypeStruct((tile_x * tile_y, members), jnp.float32),
        in_specs=[in_vmem()] * 2,
        out_specs=in_vmem(),
        scratch_shapes=[
            pltpu.VMEM((high_x, high_y, members), jnp.float32),
            pltpu.VMEM((high_x, high_y, members), jnp.float32),
            pltpu.VMEM((kinds * high_x, high_y, members), jnp.float32),
        ],
        compiler_params=grant(16),
        cost_estimate=pl.CostEstimate(
            flops=20 * work, bytes_accessed=8 * high_x * high_y * members, transcendentals=work
        ),
    )(padded, columns)


def share(rows, axis, count, groups=None):
    height, width = rows.shape
    copies = jnp.broadcast_to(rows[None], (count, height, width)).reshape(count * height, width)
    return lax.all_to_all(copies, axis, 0, 0, axis_index_groups=groups, tiled=True)


def along_planes(narrow, wide):
    ys, xs, cs = GY_FACTORS[narrow]

    def at(y, x, c):
        return (y * xs + x) * cs + c

    planes = [
        [z * narrow + at(y, x, c) for y in range(ys) for z in range(wide)]
        for x in range(xs)
        for c in range(cs)
    ]
    lines = [[at(y, x, c) for x in range(xs)] for y in range(ys) for c in range(cs)]
    across = [(i, i ^ 1) for i in range(narrow)]
    return planes, lines, across


def gather_kernel(rows_ref, rank_ref, first_ref, rest_ref):
    slots = rows_ref.shape[0]
    copies, room = first_ref.shape[0], first_ref.shape[1]
    rank = lax.broadcasted_iota(jnp.int32, (slots, slots), 0).astype(jnp.float32)
    pick = (rank == rank_ref[...]).astype(jnp.float32).astype(jnp.bfloat16)
    left = rows_ref[...]
    packed = jnp.zeros_like(left)
    for _ in range(3):
        part = left.astype(jnp.bfloat16)
        packed = packed + jnp.dot(pick, part, preferred_element_type=jnp.float32)
        left = left - part.astype(jnp.float32)
    for copy in range(copies):
        first_ref[copy] = packed[:room]
    rest_ref[...] = packed[room:]


def gather(rows, rank, copies, room):
    slots, members = rows.shape
    return pl.pallas_call(
        gather_kernel,
        name="gather",
        out_shape=(
            jax.ShapeDtypeStruct((copies, room, members), jnp.float32),
            jax.ShapeDtypeStruct((slots - room, members), jnp.float32),
        ),
        in_specs=[in_vmem()] * 2,
        out_specs=(in_vmem(),) * 2,
        compiler_params=grant(8),
    )(rows, rank)


def unread(shape):
    array = jax.ShapeDtypeStruct(shape, jnp.float32)
    anywhere = pl.BlockSpec(memory_space=pl.ANY)
    return pl.pallas_call(
        lambda *refs: None, name="unread", out_shape=(array, array), out_specs=(anywhere, anywhere)
    )()


def share_all(copies, rank, crowded, wide, narrow, beside):
    xs = GY_FACTORS[narrow][1]
    planes, lines, across = along_planes(narrow, wide)
    rows = lax.all_to_all(copies, ("gx", "gy"), 0, 0, axis_index_groups=planes, tiled=True)
    rows = rows.reshape(-1, rows.shape[-1])
    slots, members = rows.shape
    rows, rank, crowded, beside = lax.optimization_barrier((rows, rank, crowded, beside))
    first, rest = gather(rows, rank, xs, slots // 2)
    near = lax.all_to_all(first.reshape(-1, members), "gy", 0, 0, axis_index_groups=lines, tiled=True)
    far = lax.ppermute(near, "gy", across)

    def send(rest):
        near = share(rest, "gy", xs, lines)
        return near, lax.ppermute(near, "gy", across)

    def skip(rest):
        return unread((xs * rest.shape[0], members))

    more_near, more_far = lax.cond(crowded, send, skip, rest)
    return (near, far, more_near, more_far), beside


def local_cells(tile_id, obs_owner, obs_cell, obs_batch):
    span = 2048
    order = jnp.arange(obs_owner.shape[0], dtype=jnp.int32)
    key = (order * span + obs_cell)[None, :]
    batches = jnp.arange(BATCHES, dtype=jnp.int32)[:, None]
    mine = (obs_owner == tile_id)[None, :] & (obs_batch[None, :] == batches)
    first = jnp.min(jnp.where(mine, key, obs_owner.shape[0] * span), 1)
    last = jnp.max(jnp.where(mine, key, 0), 1)
    return jnp.stack([first, last], 1).reshape(-1) & (span - 1)


def locate(wide, narrow, owner):
    _, xs, cs = GY_FACTORS[narrow]
    row, col = owner // narrow, owner % narrow
    y, x, c = col // (xs * cs), col // cs % xs, col % cs
    return c * xs + x, y * wide + row


def sort(wide, narrow, owner, batch):
    count = owner.shape[0]
    ys, xs, cs = GY_FACTORS[narrow]
    plane, tile = locate(wide, narrow, owner)
    place = (batch * (xs * cs) + plane) * (ys * wide) + tile
    key = place * count + jnp.arange(count, dtype=jnp.int32)
    ahead = key[:, None] < key[None, :]
    position = jnp.sum(ahead.astype(jnp.int32), 0)
    second = jnp.sum((ahead & (place[:, None] == place[None, :])).astype(jnp.int32), 0)
    return position, second


def arrange(
    row_index, col_index, tile_x, tile_y, wide, narrow, owner, cell, batch, value, var, position, second
):
    count = owner.shape[0]
    ys, xs, cs = GY_FACTORS[narrow]
    number = xs * cs
    slots = ys * wide * BATCHES * CAP
    room = slots // 2
    side = col_index % cs
    own_plane = side * xs + col_index // cs % xs
    order = jnp.arange(count, dtype=jnp.int32)
    plane, tile = locate(wide, narrow, owner)
    group = batch * number + plane
    place = group * (ys * wide) + tile
    groups = jnp.arange(BATCHES * number, dtype=jnp.int32)
    member = (group[None, :] == groups[:, None]).astype(jnp.int32)
    held = jnp.sum(member, 1)
    before = jnp.sum(jnp.where(groups[None, :] < groups[:, None], held[None, :], 0), 1)
    base = jnp.concatenate([jnp.zeros((number,), jnp.int32), held[:number]])
    rank = position + jnp.sum(member * (base - before)[:, None], 0)
    crowded = jnp.any(held[:number] + held[number:] > room)
    slot = tile * (BATCHES * CAP) + batch * CAP + second
    here = (plane == own_plane)[None, :] & (
        slot[None, :] == jnp.arange(slots, dtype=jnp.int32)[:, None]
    )
    own_rank = (jnp.sum(jnp.where(here, rank[None, :] + 1, 0), 1) - 1).astype(jnp.float32)[None, :]
    shelf = ((plane // xs) ^ side) * xs + plane % xs
    source = jnp.where(
        rank < room,
        shelf * room + rank,
        number * room + shelf * (slots - room) + (rank - room),
    )
    px = owner // narrow * tile_x + cell // tile_y - row_index * tile_x
    py = owner % narrow * tile_y + cell % tile_y - col_index * tile_y
    pick = (position[None, :] == order[:, None]).astype(jnp.float32)
    table = jnp.stack(
        [
            source.astype(jnp.float32),
            place.astype(jnp.float32),
            px.astype(jnp.float32),
            py.astype(jnp.float32),
            value,
            var,
        ],
        0,
    )
    table = lax.dot_general(table, pick, (((1,), (1,)), ((), ())), precision=lax.Precision.HIGHEST)
    source = (table[0] + 0.5).astype(jnp.int32)
    source = jnp.concatenate([source, jnp.broadcast_to(crowded.astype(jnp.int32), (8,))])
    place = table[1]
    edge = jnp.full((1,), -1.0, jnp.float32)
    follows = (place == jnp.concatenate([edge, place[:-1]])).astype(jnp.float32)
    leads = (place == jnp.concatenate([place[1:], edge])).astype(jnp.float32)

    def mate(row):
        zero = jnp.zeros((1,), jnp.float32)
        return leads * jnp.concatenate([row[1:], zero]) + follows * jnp.concatenate(
            [zero, row[:-1]]
        )

    rows = jnp.stack(
        [
            table[4],
            table[5],
            mate(table[4]),
            mate(table[5]) + (1.0 - leads - follows),
            leads,
            follows,
            table[2],
            table[3],
        ],
        0,
    )
    return source, rows, own_rank, crowded


def split(value):
    high = value.astype(jnp.bfloat16)
    low = (value - high.astype(jnp.float32)).astype(jnp.bfloat16)
    return high, low


def assimilate_kernel(
    tile_x,
    tile_y,
    reach_x,
    reach_y,
    source_ref,
    rows_ref,
    cols_ref,
    near_ref,
    far_ref,
    more_near_ref,
    more_far_ref,
    field_ref,
    out_ref,
    shared_ref,
    obs_ref,
    gain_a,
    gain_b,
    change_a,
    change_b,
    taper_x,
    taper_y,
    sems,
):
    count, members = obs_ref.shape
    half = count // BATCHES
    scale_x = -0.5 / (reach_x * reach_x)
    scale_y = -0.5 / (reach_y * reach_y)

    first, more = near_ref.shape[0], more_near_ref.shape[0]
    shared_ref[:first, :] = near_ref[...]
    shared_ref[first : 2 * first, :] = far_ref[...]

    @pl.when(source_ref[count] > 0)
    def _():
        copies = [
            pltpu.make_async_copy(
                part_ref, shared_ref.at[pl.ds(2 * first + i * more, more)], sems.at[i]
            )
            for i, part_ref in enumerate((more_near_ref, more_far_ref))
        ]
        for copy in copies:
            copy.start()
        for copy in copies:
            copy.wait()

    def fetch(index, carry):
        obs_ref[pl.ds(index, 1), :] = shared_ref[pl.ds(source_ref[index], 1), :]
        return carry

    lax.fori_loop(0, count, fetch, 0, unroll=8)

    def prepare(batch):
        low = batch * half
        prior = obs_ref[low : low + half, :]
        cols = cols_ref[low : low + half, :]
        value, var, mate_value, mate_var = (cols[:, i : i + 1] for i in range(4))
        leads, follows = cols[:, 4:5], cols[:, 5:6]
        mean = jnp.mean(prior, 1, keepdims=True)
        own = prior - mean
        after = pltpu.roll(prior, half - 1, 0)
        before = pltpu.roll(prior, 1, 0)
        mate_prior = jnp.where(leads > 0.0, after, before)
        mate_mean = jnp.mean(mate_prior, 1, keepdims=True)
        paired = leads + follows
        mate = (mate_prior - mate_mean) * paired
        own_own = jnp.sum(own * own, 1, keepdims=True)
        own_mate = jnp.sum(own * mate, 1, keepdims=True)
        rest = mate - own * (own_mate / jnp.maximum(own_own, 1e-30))
        area = own_own * jnp.sum(rest * rest, 1, keepdims=True)
        mate_mate = jnp.sum(mate * mate, 1, keepdims=True)
        floor = jnp.float32(members - 1)
        own_floor, mate_floor = floor * var, floor * mate_var
        det = own_floor * mate_floor + own_floor * mate_mate + mate_floor * own_own + area
        own_part = (mate_floor * own_own + area) / det
        mate_part = own_floor * own_mate / det
        shift = own_part * (value - mean) + mate_part * paired * (mate_value - mate_mean)
        change = shift - 0.5 * (own_part * own + mate_part * mate)
        gain = (own / (own_own + EPS)).T
        high, low_part = split(gain)
        gain_a[batch, :members, :] = high
        gain_a[batch, members:, :] = high
        gain_b[batch] = low_part
        high, low_part = split(change)
        change_a[batch, :, :members] = high
        change_a[batch, :, members:] = low_part
        change_b[batch] = high

    def increment(batch, cells, taper):
        anomaly = cells - jnp.mean(cells, 1, keepdims=True)
        high, low = split(anomaly)
        covary = jnp.dot(
            jnp.concatenate([high, low], 1), gain_a[batch], preferred_element_type=jnp.float32
        ) + jnp.dot(high, gain_b[batch], preferred_element_type=jnp.float32)
        high, low = split(covary * taper)
        both = jnp.dot(high, change_a[batch], preferred_element_type=jnp.float32)
        rest = jnp.dot(low, change_b[batch], preferred_element_type=jnp.float32)
        return cells + (both[:, :members] + both[:, members:] + rest)

    def update_field(batch, from_ref):
        low = batch * half
        obs_x = rows_ref[6:7, low : low + half]
        obs_y = rows_ref[7:8, low : low + half]
        at_x = lax.broadcasted_iota(jnp.int32, (tile_x, half), 0).astype(jnp.float32) - obs_x
        at_y = lax.broadcasted_iota(jnp.int32, (tile_y, half), 0).astype(jnp.float32) - obs_y
        taper_x[...] = jnp.exp(scale_x * (at_x * at_x))
        taper_y[...] = jnp.exp(scale_y * (at_y * at_y))

        for first in range(0, tile_x, GROUP):
            where = slice(first * tile_y, (first + GROUP) * tile_y)
            taper = jnp.concatenate(
                [taper_x[first + i : first + i + 1, :] * taper_y[...] for i in range(GROUP)], 0
            )
            out_ref[where, :] = increment(batch, from_ref[where, :], taper)

    prepare(0)
    chunk = min(half, 256)
    for start in range(half, count, chunk):
        gap_x = cols_ref[start : start + chunk, 6:7] - rows_ref[6:7, :half]
        gap_y = cols_ref[start : start + chunk, 7:8] - rows_ref[7:8, :half]
        taper = jnp.exp(scale_x * (gap_x * gap_x) + scale_y * (gap_y * gap_y))
        obs_ref[start : start + chunk, :] = increment(0, obs_ref[start : start + chunk, :], taper)
    prepare(1)
    update_field(0, field_ref)
    update_field(1, out_ref)


def assimilate(source, rows, cols, shared, field, tile_x, tile_y, reach_x, reach_y):
    cells, members = field.shape
    count = rows.shape[1]
    half = count // BATCHES
    near, far, *more = shared
    more = [pltpu.with_memory_space_constraint(part, pltpu.HBM) for part in more]
    return pl.pallas_call(
        functools.partial(assimilate_kernel, tile_x, tile_y, reach_x, reach_y),
        name="assimilate",
        out_shape=jax.ShapeDtypeStruct((cells, members), jnp.float32),
        in_specs=[in_smem()]
        + [in_vmem()] * 4
        + [pl.BlockSpec(memory_space=pl.ANY)] * 2
        + [in_vmem()],
        out_specs=in_vmem(),
        scratch_shapes=[
            pltpu.VMEM((sum(part.shape[0] for part in shared), members), jnp.float32),
            pltpu.VMEM((count, members), jnp.float32),
            pltpu.VMEM((BATCHES, 2 * members, half), jnp.bfloat16),
            pltpu.VMEM((BATCHES, members, half), jnp.bfloat16),
            pltpu.VMEM((BATCHES, half, 2 * members), jnp.bfloat16),
            pltpu.VMEM((BATCHES, half, members), jnp.bfloat16),
            pltpu.VMEM((tile_x, half), jnp.float32),
            pltpu.VMEM((tile_y, half), jnp.float32),
            pltpu.SemaphoreType.DMA((2,)),
        ],
        compiler_params=grant(40),
    )(source, rows, cols, near, far, *more, field)


def per_device(ensemble, coefficients, obs_owner, obs_cell, obs_batch, obs_value, obs_var):
    wide = lax.axis_size("gx")
    narrow = lax.axis_size("gy")
    row_index = lax.axis_index("gx")
    col_index = lax.axis_index("gy")
    tile_x, tile_y, members = ensemble.shape
    reach_x = tile_x * wide / 2.0
    reach_y = tile_y * narrow / 2.0
    cells = local_cells(row_index * narrow + col_index, obs_owner, obs_cell, obs_batch)
    position, second = sort(wide, narrow, obs_owner, obs_batch)
    first, last, coefs = pack_x(ensemble, coefficients)
    before, after = exchange(last, first, "gx")
    first, last = pack_y(ensemble, coefs, before, after)
    left, right = exchange(last, first, "gy")
    padded, columns, priors = look(
        wide * GY_FACTORS[narrow][0], cells, ensemble, coefs, before, after, left, right
    )
    priors, position, second = lax.optimization_barrier((priors, position, second))
    source, rows, rank, crowded = arrange(
        row_index,
        col_index,
        tile_x,
        tile_y,
        wide,
        narrow,
        obs_owner,
        obs_cell,
        obs_batch,
        obs_value,
        obs_var,
        position,
        second,
    )
    field = forecast(coefficients.shape[0], padded, columns)
    shared, (field, source, rows, cols) = share_all(
        priors, rank, crowded, wide, narrow, (field, source, rows, rows.T)
    )
    field = assimilate(
        source, rows, cols, shared, field, tile_x, tile_y, reach_x, reach_y
    )
    return field.reshape(tile_x, tile_y, members)


def solution(mesh):
    placed = (P("gx", "gy", None), P(None, "gx", "gy"), P(), P(), P(), P(), P())
    return jax.shard_map(
        per_device, mesh=mesh, in_specs=placed, out_specs=P("gx", "gy", None), check_vma=False
    )
```
